32 devices in a mesh: head: 4 (over z), blk: 8 (over y, x, core).
Axes of the slice: x: 2, y: 2, z: 4, core: 2. Of those that a mesh axis runs over, the one named last changes fastest.
Arguments:
- tokens: bfloat16 [4096, 1024], P(('blk', 'head')), may hold values from -6 to 6
- segments: int32 [4096], replicated, may hold values from 0 to 8, as said below
- routes: int32 [4096, 8], P(('blk', 'head')), may hold values from 0 to 31, all different within a row; in each aligned block of 128 rows (0 to 127, 128 to 255, ...) at most 40 rows name the same one
- w_query: bfloat16 [2, 1024, 1024], P(None, ('head', 'blk')), may hold values from -0.1875 to 0.1875
- w_key: bfloat16 [2, 1024, 512], P(None, ('head', 'blk')), may hold values from -0.25 to 0.25
- w_value: bfloat16 [2, 1024, 512], P(None, ('head', 'blk')), may hold values from -0.1875 to 0.1875
- w_out: bfloat16 [2, 1024, 1024], P(None, ('head', 'blk')), may hold values from -0.375 to 0.375
- w_router: bfloat16 [2, 1024, 32], P(None, ('head', 'blk')), may hold values from -0.25 to 0.25
- gain_attn: bfloat16 [2, 1024], P(None, ('head', 'blk')), may hold values from 0.5 to 1.5
- gain_ffn: bfloat16 [2, 1024], P(None, ('head', 'blk')), may hold values from 0.5 to 1.5
- w_gate: bfloat16 [2, 32, 1024, 512], P(None, 'head', 'blk'), may hold values from -0.1875 to 0.1875
- w_up: bfloat16 [2, 32, 1024, 512], P(None, 'head', 'blk'), may hold values from -0.1875 to 0.1875
- w_down: bfloat16 [2, 32, 1024, 512], P(None, 'head', 'blk'), may hold values from -0.5 to 0.5
- cotangent: bfloat16 [4096, 1024], P(('blk', 'head')), may hold values from -6 to 6
Outputs:
- layers_out: float32 [4096, 1024], P(('blk', 'head'))
- grad_tokens: float32 [4096, 1024], P(('blk', 'head'))
- grad_query: float32 [2, 1024, 1024], P(None, ('head', 'blk'))
- grad_key: float32 [2, 1024, 512], P(None, ('head', 'blk'))
- grad_value: float32 [2, 1024, 512], P(None, ('head', 'blk'))
- grad_out: float32 [2, 1024, 1024], P(None, ('head', 'blk'))
- grad_router: float32 [2, 1024, 32], P(None, ('head', 'blk'))
- grad_gain_attn: float32 [2, 1024], P(None, ('head', 'blk'))
- grad_gain_ffn: float32 [2, 1024], P(None, ('head', 'blk'))
- grad_gate: float32 [2, 32, 1024, 512], P(None, 'head', 'blk')
- grad_up: float32 [2, 32, 1024, 512], P(None, 'head', 'blk')
- grad_down: float32 [2, 32, 1024, 512], P(None, 'head', 'blk')
The draws below stay inside these ranges and needn't reach their ends.
Inputs may be any that keep to these rules, and one draw needn't show every extreme that they name: `segments`: documents are contiguous and lie inside the sequences of 4096 tokens: segment numbers never fall along the stream and no document crosses a multiple of 4096. In every sequence the longest document has exactly 2560 tokens. `routes`: each token names 8 different experts. Within the rows of one device no expert is named more than 40 times, and that many is reached.
All inputs are finite; a program needn't handle non-finite values.
Results may differ from the reference program's by a relative error of at most 0.04.
Values may be sent and summed in bfloat16 or wider, within the bound.
No kernel may reach another device: no remote copies, remote signals or barrier semaphores. Data moves between devices by JAX's collectives and lax.ppermute only.
A program may use at most 256 MiB of HBM per device.

```python
import math
import jax
import jax.numpy as jnp
import numpy as np
from jax import lax

D = 1024
H = 16
KVH = 8
HD = 64
E = 32
FF = 512
TOPK = 8
LAYERS = 2
TOK_DEV = 128
TOKENS = 4096
SEQ = 4096
CAP = 40
SPAN = 2560


def draw_segments(key, part):
    seq_count = TOKENS // SEQ
    remain = SEQ - SPAN
    key_cuts, key_side = jax.random.split(jax.random.fold_in(key, 11))
    cuts = jax.random.randint(key_cuts, (seq_count, 1, 7), 1, remain)
    long_first = jax.random.randint(key_side, (seq_count, 1), 0, 2)
    places = jnp.arange(SEQ, dtype=jnp.int32)[None, :]
    after_long = places - SPAN
    first_case = jnp.where(places < SPAN, 0, 1 + jnp.sum((cuts <= after_long[:, :, None]).astype(jnp.int32), axis=-1))
    last_case = jnp.where(places >= remain, 8, jnp.sum((cuts <= places[:, :, None]).astype(jnp.int32), axis=-1))
    local = jnp.where(long_first == 1, first_case, last_case)
    numbers = jnp.arange(seq_count, dtype=jnp.int32)[:, None] * 9 + local
    return numbers.reshape(-1).astype(jnp.int32)


def raised(values, own_key, source, target, parts, factor):
    def block_of(position):
        return (jnp.arange(values.shape[position]) // (values.shape[position] // parts)).reshape((-1,) + (1,) * (values.ndim - 1 - position))

    one_side = jax.random.permutation(own_key, parts)[block_of(target)]
    far = (block_of(target) + parts // 2) % parts
    return jnp.where((block_of(source) == one_side) | (block_of(source) == far), factor * values, values)


def steps_of(own_key, dims, cuts, smallest, high):
    def one(axis_at, shards_of):
        heights = jax.random.uniform(jax.random.fold_in(jax.random.fold_in(own_key, 6), axis_at), (shards_of,), jnp.float32, smallest / len(cuts), high / len(cuts))
        return jnp.repeat(jnp.exp(heights), dims[axis_at] // shards_of).reshape((-1,) + (1,) * (len(dims) - axis_at - 1))

    loudness = one(*cuts[0])
    for cut in cuts[1:]:
        loudness = loudness * one(*cut)
    return loudness


def routed_block(stream_key, own, number, rows, count, top, limit, skew):
    order = jax.random.permutation(stream_key, count)
    packed, common = shares(count, rows * top, limit, skew, True), shares(count, rows * top, limit, skew, False)
    places = jnp.arange(count)

    def named(lengths, offset_by):
        used = int((lengths > 0).sum())
        fixed = max(1, used // 4)
        moved = fixed + (places - fixed + offset_by * (used - fixed)) % max(1, count - fixed)
        return jnp.zeros((count,), jnp.int32).at[order[jnp.where(places < fixed, places, moved)]].set(jnp.asarray(lengths, jnp.int32))

    lengths = jnp.where(number % 4 == 0, named(packed, number // 4), named(common, number - number // 4 - 1))
    mixed = jax.random.permutation(jax.random.fold_in(own, 3), count)
    donor, receiver = mixed[0:count // 2 * 2:2], mixed[1:count // 2 * 2:2]
    margin = jnp.minimum(lengths[donor] - 1, limit - lengths[receiver]) // 2
    margin = jnp.where((donor == order[0]) | (receiver == order[0]) | (lengths[receiver] == 0), 0, jnp.maximum(margin, 0))
    moved = jax.random.randint(jax.random.fold_in(own, 4), (count // 2,), 0, 1 << 20) % (margin + 1)
    lengths = lengths.at[donor].add(-moved).at[receiver].add(moved)
    members = jnp.searchsorted(jnp.cumsum(lengths), jnp.arange(rows * top), side="right").astype(jnp.int32)
    table = members.reshape(top, rows).T
    table = table[jax.random.permutation(jax.random.fold_in(own, 1), rows)]
    offset_by = jax.random.randint(jax.random.fold_in(own, 2), (rows, 1), 0, top)
    return jnp.take_along_axis(table, (jnp.arange(top)[None, :] + offset_by) % top, axis=1)


def shares(number_of, total, limit, slope, full):
    portions = [(1 << 20) // math.isqrt(grade ** slope) + 1 for grade in range(1, number_of + 1)]
    largest = limit if full else min(limit, max(-(-total // number_of), total * portions[0] // sum(portions)))
    least = 1 if total - largest >= number_of - 1 else 0
    holding, spare = [largest] + [least] * (number_of - 1), total - largest - least * (number_of - 1)
    while spare > 0:
        free = [i for i in range(1, number_of) if holding[i] < largest] or [i for i in range(1, number_of) if holding[i] < limit]
        whole, left = sum([portions[i] for i in free]), spare
        for i in free:
            addition = min(limit - holding[i], max(1, left * portions[i] // whole), spare)
            holding[i] = holding[i] + addition
            spare = spare - addition
    return np.array(holding)


def bell_draw(stream_key, dims, scale, bound, shards=(), kind=jnp.bfloat16):
    entries = jax.random.normal(stream_key, dims, jnp.float32) * scale
    if len(shards) > 0:
        entries = steps_of(stream_key, dims, shards, -0.22, 0.18) * entries
    return jnp.clip(entries, min=-bound, max=bound).astype(kind)


def bell_draw_with(own_key, shape, deviation, most, pieces, heavy, kind=jnp.bfloat16):
    values = deviation * jax.random.normal(own_key, shape, jnp.float32)
    if pieces:
        values = values * steps_of(own_key, shape, pieces, -0.22, 0.18)
    return jnp.clip(raised(values, jax.random.fold_in(own_key, 3), *heavy), -most, most).astype(kind)


def setup_inputs(seed: int = 0) -> dict:
    splits = jax.random.split(jax.random.key(seed), 15)
    tokens = bell_draw_with(splits[0], (TOKENS, D), 1.0, 6.0, ((0, 32),), (0, 1, 32, 2.75))
    segments = draw_segments(jax.random.fold_in(splits[14], 71), 0)
    routes_keys = jax.random.split(jax.random.fold_in(splits[2], 1), TOKENS // TOK_DEV)
    routes_turns = jax.random.permutation(jax.random.fold_in(splits[2], 3), TOKENS // TOK_DEV)
    routes = jax.vmap(lambda own, number: routed_block(jax.random.fold_in(splits[2], 2), own, number, TOK_DEV, E, TOPK, CAP, 1))(routes_keys, routes_turns).reshape((TOKENS, TOPK))
    w_query = bell_draw(splits[3], (LAYERS, D, H * HD), D ** -0.5, 0.1875, ((1, 32),))
    w_key = bell_draw(splits[4], (LAYERS, D, KVH * HD), (D // 2) ** -0.5, 0.25, ((1, 32),))
    w_value = bell_draw(splits[5], (LAYERS, D, KVH * HD), D ** -0.5, 0.1875, ((1, 32),))
    w_out = bell_draw(splits[6], (LAYERS, H * HD, D), (D // 4) ** -0.5, 0.375, ((1, 32),))
    w_router = bell_draw(splits[7], (LAYERS, D, E), (D // 2) ** -0.5, 0.25, ((1, 32),))
    gain_attn = jnp.clip(1.0 + 0.1 * jax.random.normal(splits[8], (LAYERS, D), jnp.float32), 0.5, 1.5).astype(jnp.bfloat16)
    gain_ffn = jnp.clip(1.0 + 0.1 * jax.random.normal(splits[9], (LAYERS, D), jnp.float32), 0.5, 1.5).astype(jnp.bfloat16)
    w_gate = bell_draw(splits[10], (LAYERS, E, D, FF), D ** -0.5, 0.1875, ((1, 4), (2, 8)))
    w_up = bell_draw(splits[11], (LAYERS, E, D, FF), D ** -0.5, 0.1875, ((1, 4), (2, 8)))
    w_down = bell_draw(splits[12], (LAYERS, E, D, FF), (FF // 4) ** -0.5, 0.5, ((1, 4), (2, 8)))
    cotangent = bell_draw(splits[13], (TOKENS, D), 1.0, 6.0, ((0, 32),))
    return dict(tokens=tokens, segments=segments, routes=routes, w_query=w_query, w_key=w_key, w_value=w_value, w_out=w_out, w_router=w_router, gain_attn=gain_attn, gain_ffn=gain_ffn, w_gate=w_gate, w_up=w_up, w_down=w_down, cotangent=cotangent)


@jax.custom_vjp
def low(v):
    return lax.optimization_barrier(v.astype(jnp.bfloat16)).astype(jnp.float32)

@jax.custom_vjp
def low_back(v):
    return v

def low_keep(v):
    return (low(v), None)

def low_pass(kept, grad):
    return (grad,)

def back_keep(v):
    return (v, None)

def back_low(kept, grad):
    return (low(grad),)
low.defvjp(low_keep, low_pass)
low_back.defvjp(back_keep, back_low)
EPSILON = 1e-06
MASKED = -1e+30
ROPE_BASE = 10000.0
PRECISE = lax.Precision.HIGHEST

def product(left, right):
    return jnp.dot(left, right, precision=PRECISE)

def rms_scale(values):
    return lax.rsqrt(lax.optimization_barrier(jnp.mean(values * values, axis=-1, keepdims=True)) + EPSILON)

def rotate(values, cosine_table, sine_table):
    half_dim = values.shape[-1] // 2
    first = values[..., :half_dim]
    second = values[..., half_dim:]
    return jnp.concatenate([first * cosine_table - second * sine_table, second * cosine_table + first * sine_table], axis=-1)

def rotary_tables(start, count, head_dim):
    half_dim = head_dim // 2
    frequency = jnp.power(ROPE_BASE, -(jnp.arange(half_dim, dtype=jnp.float32) * 2.0 / head_dim))
    places = jnp.remainder(start + jnp.arange(count, dtype=jnp.int32), SEQ)
    angles = places.astype(jnp.float32)[:, None] * frequency[None, :]
    return (jnp.cos(angles)[:, None, :], jnp.sin(angles)[:, None, :])

def attention(queries, keys, values, segments):
    groups = H // KVH
    keys_all = jnp.repeat(keys, groups, axis=1)
    values_all = jnp.repeat(values, groups, axis=1)
    score_scale = HD ** (-0.5)
    query_rows = min(512, SEQ)

    def one_block(start):
        seq_start = start // SEQ * SEQ
        query_block = lax.dynamic_slice_in_dim(queries, start, query_rows, 0)
        query_segs = lax.dynamic_slice_in_dim(segments, start, query_rows, 0)
        query_pos = start + jnp.arange(query_rows, dtype=jnp.int32)
        key_block = lax.dynamic_slice_in_dim(keys_all, seq_start, SEQ, 0)
        value_block = lax.dynamic_slice_in_dim(values_all, seq_start, SEQ, 0)
        key_segs = lax.dynamic_slice_in_dim(segments, seq_start, SEQ, 0)
        key_pos = seq_start + jnp.arange(SEQ, dtype=jnp.int32)
        allowed = (query_segs[:, None] == key_segs[None, :]) & (query_pos[:, None] >= key_pos[None, :])
        scores = jnp.einsum('qhd,khd->hqk', query_block, key_block, precision=PRECISE) * score_scale
        scores = low_back(jnp.where(allowed[None], scores, MASKED))
        probability = low(jax.nn.softmax(scores, axis=-1))
        return jnp.einsum('hqk,khd->qhd', probability, value_block, precision=PRECISE)
    blocks = lax.map(jax.checkpoint(one_block), jnp.arange(TOKENS // query_rows, dtype=jnp.int32) * query_rows)
    return blocks.reshape(TOKENS, H * HD)

def experts(normed, routes, w_gate, w_up, w_down):
    sources = TOKENS // TOK_DEV
    flat_route = routes.reshape(-1)
    route_hot = (flat_route[:, None] == jnp.arange(E, dtype=jnp.int32)[None, :]).astype(jnp.int32)
    running = jnp.cumsum(route_hot.reshape(sources, TOK_DEV * TOPK, E), axis=1).reshape(-1, E)
    slot_index = lax.optimization_barrier(jnp.sum(route_hot * (running - 1), axis=1))
    source = jnp.arange(TOKENS * TOPK, dtype=jnp.int32) // (TOK_DEV * TOPK)
    buffer_row = source * CAP + slot_index
    buffer = jnp.zeros((E, sources * CAP, D), jnp.float32).at[flat_route, buffer_row].set(jnp.repeat(normed, TOPK, axis=0))
    buffer = low_back(buffer)
    gate_pre = low_back(jnp.einsum('erd,edf->erf', buffer, w_gate, precision=PRECISE))
    up_pre = low_back(jnp.einsum('erd,edf->erf', buffer, w_up, precision=PRECISE))
    hidden = low(jax.nn.silu(gate_pre) * up_pre)
    result = low_back(low(jnp.einsum('erf,edf->erd', hidden, w_down, precision=PRECISE)))
    return result[flat_route, buffer_row].reshape(TOKENS, TOPK, D)

def one_layer(stream, segments, routes, mats, cosine_table, sine_table):
    w_query, w_key, w_value, w_out, w_router, gain_attn, gain_ffn, w_gate, w_up, w_down = mats
    normed_attn = low(stream * rms_scale(stream) * gain_attn)
    query_pre = low_back(product(normed_attn, w_query)).reshape(TOKENS, H, HD)
    key_pre = low_back(product(normed_attn, w_key)).reshape(TOKENS, KVH, HD)
    queries = low_back(low(rotate(query_pre, cosine_table, sine_table)))
    keys = low_back(low(rotate(key_pre, cosine_table, sine_table)))
    values = low_back(low(product(normed_attn, w_value))).reshape(TOKENS, KVH, HD)
    attended = low_back(low(attention(queries, keys, values, segments)))
    middle = stream + low_back(product(attended, w_out))
    normed_ffn = low(middle * rms_scale(middle) * gain_ffn)
    logits = product(normed_ffn, w_router)
    onehot = (routes[:, :, None] == jnp.arange(E, dtype=jnp.int32)[None, None, :]).astype(jnp.float32)
    chosen = lax.optimization_barrier(jnp.sum(onehot * logits[:, None, :], axis=-1))
    gate_prob = jax.nn.softmax(chosen, axis=-1)
    picked = experts(normed_ffn, routes, w_gate, w_up, w_down)
    return middle + lax.optimization_barrier(jnp.sum(gate_prob[..., None] * picked, axis=1))

def reference(tokens, segments, routes, w_query, w_key, w_value, w_out, w_router, gain_attn, gain_ffn, w_gate, w_up, w_down, cotangent):
    cosine_table, sine_table = rotary_tables(0, TOKENS, HD)
    weights = tuple((matrix.astype(jnp.float32) for matrix in (w_query, w_key, w_value, w_out, w_router, gain_attn, gain_ffn, w_gate, w_up, w_down)))

    def forward(stream, mats):
        for layer_index in range(LAYERS):
            stream = one_layer(stream, segments, routes, tuple((matrix[layer_index] for matrix in mats)), cosine_table, sine_table)
        return stream
    output, pullback = jax.vjp(forward, tokens.astype(jnp.float32), weights)
    grad_stream, grad_mats = pullback(cotangent.astype(jnp.float32))
    return (output, grad_stream, grad_mats[0], grad_mats[1], grad_mats[2], grad_mats[3], grad_mats[4], grad_mats[5], grad_mats[6], grad_mats[7], grad_mats[8], grad_mats[9])
```

```python
import jax
import jax.numpy as jnp
from jax import lax
from jax.sharding import PartitionSpec as P

D = 1024
H = 16
KVH = 8
HD = 64
E = 32
LAYERS = 2
CAP = 40
SIDE = 128


EPSILON = 1e-06
MASKED = -1e30
ROPE_BASE = 10000.0
PRECISE = lax.Precision.HIGHEST
BOTH = ("head", "blk")


def rms_scale(values):
    return lax.rsqrt(jnp.mean(values * values, axis=-1, keepdims=True) + EPSILON)


def rotate(values, cosine_table, sine_table):
    half_dim = values.shape[-1] // 2
    first = values[..., :half_dim]
    second = values[..., half_dim:]
    return jnp.concatenate(
        [first * cosine_table - second * sine_table, second * cosine_table + first * sine_table],
        axis=-1,
    )


def rotary_tables(start, count, head_dim):
    half_dim = head_dim // 2
    frequency = jnp.power(ROPE_BASE, -(jnp.arange(half_dim, dtype=jnp.float32) * 2.0 / head_dim))
    places = start + jnp.arange(count, dtype=jnp.int32)
    angles = places.astype(jnp.float32)[:, None] * frequency[None, :]
    return (jnp.cos(angles)[:, None, :], jnp.sin(angles)[:, None, :])


def dot(left, right):
    return jnp.dot(left, right, preferred_element_type=jnp.float32)


def contract_rows(left, right, precision=None):
    return lax.dot_general(
        left,
        right,
        (((0,), (0,)), ((), ())),
        preferred_element_type=jnp.float32,
        precision=precision,
    )


def contract_cols(left, right, precision=None):
    return lax.dot_general(
        left,
        right,
        (((1,), (1,)), ((), ())),
        preferred_element_type=jnp.float32,
        precision=precision,
    )


def halves(values):
    high = lax.reduce_precision(values, 8, 7)
    return (high.astype(jnp.bfloat16), (values - high).astype(jnp.bfloat16))


def norm_back(stream, scale, gain, grad_normed):
    inner = grad_normed * gain
    grad_gain = jnp.sum(grad_normed * stream * scale, axis=0)
    grad_stream = scale * inner - stream * scale * scale * scale * jnp.mean(
        stream * inner, axis=-1, keepdims=True
    )
    return (grad_stream, grad_gain)


def per_device(
    tokens,
    segments,
    routes,
    w_query,
    w_key,
    w_value,
    w_out,
    w_router,
    gain_attn,
    gain_ffn,
    w_gate,
    w_up,
    w_down,
    cotangent,
):
    head_count = lax.axis_size("head")
    cycle_count = lax.axis_size("blk")
    cycle_index = lax.axis_index("blk")
    local_tokens = tokens.shape[0]
    block_rows = local_tokens * head_count
    query_start = cycle_index * block_rows
    groups = H // KVH
    key_heads = KVH // head_count
    query_cols = H * HD // head_count
    key_cols = KVH * HD // head_count
    qkv_cols = query_cols + 2 * key_cols
    local_experts = E // head_count
    copies = cycle_count // local_experts
    copy_index = cycle_index % copies
    shard_rows = w_query.shape[1]
    slice_rows = w_gate.shape[2]
    hidden_units = w_gate.shape[3]
    score_scale = HD ** (-0.5)
    cosine_table, sine_table = rotary_tables(query_start, block_rows, HD)
    query_segs = lax.dynamic_slice_in_dim(segments, query_start, block_rows)
    query_pos = query_start + jnp.arange(block_rows, dtype=jnp.int32)
    block_last = segments.reshape(cycle_count, block_rows)[:, block_rows - 1]
    first_owner = jnp.sum(
        (block_last < query_segs[0]) & (jnp.arange(cycle_count) < cycle_index)
    ).astype(jnp.int32)

    hot = jnp.any(
        routes.T[None, :, :] == jnp.arange(E, dtype=jnp.int32)[:, None, None], axis=1
    )
    earlier = jnp.triu(jnp.ones((local_tokens, local_tokens), jnp.bfloat16), 1)
    slot = dot(hot.astype(jnp.bfloat16), earlier).astype(jnp.int32)
    picks = hot[:, None, :] & (
        slot[:, None, :] == jnp.arange(CAP, dtype=jnp.int32)[None, :, None]
    )
    picks_mat = picks.astype(jnp.bfloat16).reshape(E * CAP, local_tokens)

    def to_experts(rows):
        if copies > 1:
            mine = jnp.arange(copies)[None, :, None, None] == copy_index
            rows = jnp.where(mine, rows.reshape(E, 1, CAP, D), jnp.zeros((), rows.dtype))
            rows = rows.reshape(E * copies * CAP, D)
        return lax.all_to_all(rows, BOTH, split_axis=0, concat_axis=0, tiled=True)

    def from_experts(rows):
        rows = lax.all_to_all(rows, BOTH, split_axis=0, concat_axis=0, tiled=True)
        if copies > 1:
            rows = lax.dynamic_index_in_dim(
                rows.reshape(E, copies, CAP, D), copy_index, 1, keepdims=False
            ).reshape(E * CAP, D)
        return rows

    def by_head(values, cols):
        return values.reshape(LAYERS, shard_rows, head_count, cols)

    side = jnp.concatenate([w_router, gain_attn[..., None], gain_ffn[..., None]], axis=-1)
    side = jnp.pad(side, ((0, 0), (0, 0), (0, SIDE - side.shape[-1])))
    side = jnp.broadcast_to(side[:, :, None, :], (LAYERS, shard_rows, head_count, SIDE))
    sent = jnp.concatenate(
        [
            by_head(w_query, query_cols),
            by_head(w_key, key_cols),
            by_head(w_value, key_cols),
            side,
        ],
        axis=-1,
    )
    sent = jnp.transpose(sent, (2, 0, 1, 3))
    sent = lax.all_to_all(sent, "head", split_axis=0, concat_axis=0, tiled=True)
    attn_all = lax.all_gather(sent, "blk", axis=0, tiled=False)
    attn_all = jnp.transpose(attn_all, (2, 1, 0, 3, 4)).reshape(LAYERS, D, qkv_cols + SIDE)
    out_all = lax.all_gather(w_out, "blk", axis=1, tiled=True)

    def gather_experts(layer_index):
        mats = jnp.stack([w_gate[layer_index], w_up[layer_index], w_down[layer_index]], axis=1)
        mats = jnp.repeat(mats, copies, axis=0)
        mats = lax.all_to_all(mats, "blk", split_axis=0, concat_axis=0, tiled=True)
        return jnp.transpose(mats, (1, 0, 2, 3)).reshape(3, D, hidden_units)

    def scatter_experts(grads):
        grads = jnp.stack(grads).astype(jnp.bfloat16)
        grads = grads.reshape(3, cycle_count, slice_rows, hidden_units)
        grads = jnp.transpose(grads, (1, 0, 2, 3))
        grads = lax.all_to_all(grads, "blk", split_axis=0, concat_axis=0, tiled=True)
        grads = grads.reshape(local_experts, copies, 3, slice_rows, hidden_units)
        grads = jnp.sum(grads.astype(jnp.float32), axis=1)
        return (grads[:, 0], grads[:, 1], grads[:, 2])

    def sum_over_head(partial):
        parts = lax.all_to_all(
            partial.astype(jnp.bfloat16), "head", split_axis=0, concat_axis=0, tiled=True
        ).reshape(head_count, local_tokens, D)
        return jnp.sum(parts.astype(jnp.float32), axis=0)

    def block_mask(key_owner):
        key_start = key_owner * block_rows
        key_segs = lax.dynamic_slice_in_dim(segments, key_start, block_rows)
        key_pos = key_start + jnp.arange(block_rows, dtype=jnp.int32)
        return (query_segs[:, None] == key_segs[None, :]) & (
            query_pos[:, None] >= key_pos[None, :]
        )

    def key_block(keys_all, key_owner):
        chosen_rows = lax.dynamic_slice_in_dim(keys_all, key_owner * block_rows, block_rows)
        return (
            chosen_rows[:, :key_cols].reshape(block_rows, key_heads, HD),
            chosen_rows[:, key_cols:].reshape(block_rows, key_heads, HD),
        )

    def block_scores(query_four, key_part, allowed):
        scores = (
            jnp.einsum("qcgd,kcd->cgqk", query_four, key_part, preferred_element_type=jnp.float32)
            * score_scale
        )
        return jnp.where(allowed, scores, MASKED)

    def attend(queries, keys_all):
        query_four = queries.reshape(block_rows, key_heads, groups, HD)

        def visit(key_owner, state_in):
            running_max, running_sum, weighted = state_in
            allowed = block_mask(key_owner)
            key_part, value_part = key_block(keys_all, key_owner)
            scores = block_scores(query_four, key_part, allowed)
            new_max = jnp.maximum(running_max, jnp.max(scores, axis=-1))
            exponent = jnp.where(allowed, jnp.exp(scores - new_max[..., None]), 0.0)
            factor = jnp.exp(running_max - new_max)
            running_sum = running_sum * factor + jnp.sum(exponent, axis=-1)
            weighted = weighted * jnp.transpose(factor, (2, 0, 1))[..., None] + jnp.einsum(
                "cgqk,kcd->qcgd",
                exponent.astype(jnp.bfloat16),
                value_part,
                preferred_element_type=jnp.float32,
            )
            return (new_max, running_sum, weighted)

        start_state = (
            jnp.full((key_heads, groups, block_rows), MASKED, jnp.float32),
            jnp.zeros((key_heads, groups, block_rows), jnp.float32),
            jnp.zeros((block_rows, key_heads, groups, HD), jnp.float32),
        )
        running_max, running_sum, weighted = lax.fori_loop(
            first_owner, cycle_index + 1, visit, start_state
        )
        attended = (
            (weighted / jnp.transpose(running_sum, (2, 0, 1))[..., None])
            .astype(jnp.bfloat16)
            .reshape(block_rows, query_cols)
        )
        return (attended, running_max + jnp.log(running_sum))

    def attend_back(queries, keys_all, attended, log_total, grad_attended):
        query_four = queries.reshape(block_rows, key_heads, groups, HD)
        grad_four = grad_attended.reshape(block_rows, key_heads, groups, HD)
        row_delta = jnp.transpose(
            jnp.sum(
                grad_four.astype(jnp.float32)
                * attended.reshape(block_rows, key_heads, groups, HD).astype(jnp.float32),
                axis=-1,
            ),
            (1, 2, 0),
        )

        def visit(key_owner, state_in):
            grad_query, key_grads = state_in
            allowed = block_mask(key_owner)
            key_part, value_part = key_block(keys_all, key_owner)
            scores = block_scores(query_four, key_part, allowed)
            probability = jnp.where(allowed, jnp.exp(scores - log_total[..., None]), 0.0)
            grad_value = jnp.einsum(
                "cgqk,qcgd->kcd",
                probability.astype(jnp.bfloat16),
                grad_four,
                preferred_element_type=jnp.float32,
            )
            grad_prob = jnp.einsum(
                "qcgd,kcd->cgqk", grad_four, value_part, preferred_element_type=jnp.float32
            )
            grad_scores = (probability * (grad_prob - row_delta[..., None])).astype(jnp.bfloat16)
            grad_query = grad_query + jnp.einsum(
                "cgqk,kcd->qcgd", grad_scores, key_part, preferred_element_type=jnp.float32
            )
            grad_key = (
                jnp.einsum(
                    "cgqk,qcgd->kcd", grad_scores, query_four, preferred_element_type=jnp.float32
                )
                * score_scale
            )
            stacked = jnp.concatenate(
                [grad_key.reshape(block_rows, key_cols), grad_value.reshape(block_rows, key_cols)],
                axis=1,
            ).astype(jnp.bfloat16)
            key_grads = lax.dynamic_update_slice_in_dim(
                key_grads, stacked, key_owner * block_rows, 0
            )
            return (grad_query, key_grads)

        start_state = (
            jnp.zeros((block_rows, key_heads, groups, HD), jnp.float32),
            jnp.zeros((cycle_count * block_rows, 2 * key_cols), jnp.bfloat16),
        )
        grad_query, key_grads = lax.fori_loop(first_owner, cycle_index + 1, visit, start_state)
        key_grads = lax.all_to_all(key_grads, "blk", split_axis=0, concat_axis=0, tiled=True)
        key_grads = jnp.sum(
            key_grads.reshape(cycle_count, block_rows, 2 * key_cols).astype(jnp.float32), axis=0
        ).astype(jnp.bfloat16)
        grad_query = (grad_query * score_scale).astype(jnp.bfloat16)
        return (grad_query.reshape(block_rows, query_cols), key_grads)

    stream = tokens.astype(jnp.float32)
    saved = []
    for layer_index in range(LAYERS):
        qkv_mat = attn_all[layer_index, :, :qkv_cols]
        side_all = attn_all[layer_index, :, qkv_cols:]
        router = side_all[:, :E]
        gain_first = side_all[:, E].astype(jnp.float32)
        gain_second = side_all[:, E + 1].astype(jnp.float32)
        out_mat = out_all[layer_index]
        gate_mat, up_mat, down_mat = gather_experts(layer_index)
        scale_first = rms_scale(stream)
        normed_attn = (stream * scale_first * gain_first).astype(jnp.bfloat16)
        normed_block = lax.all_gather(normed_attn, "head", axis=0, tiled=True)
        qkv_pre = dot(normed_block, qkv_mat)
        query_pre = qkv_pre[:, :query_cols].reshape(block_rows, H // head_count, HD)
        key_pre = qkv_pre[:, query_cols : query_cols + key_cols].reshape(block_rows, key_heads, HD)
        queries = (
            rotate(query_pre, cosine_table, sine_table)
            .astype(jnp.bfloat16)
            .reshape(block_rows, query_cols)
        )
        key_rot = rotate(key_pre, cosine_table, sine_table).reshape(block_rows, key_cols)
        key_value = jnp.concatenate(
            [key_rot, qkv_pre[:, query_cols + key_cols :]], axis=1
        ).astype(jnp.bfloat16)
        keys_all = lax.all_gather(key_value, "blk", axis=0, tiled=True)
        attended, log_total = attend(queries, keys_all)
        middle = stream + sum_over_head(dot(attended, out_mat))
        scale_second = rms_scale(middle)
        normed_ffn = (middle * scale_second * gain_second).astype(jnp.bfloat16)
        logits = lax.dot_general(
            router, normed_ffn, (((0,), (1,)), ((), ())), preferred_element_type=jnp.float32
        )
        top = jnp.max(jnp.where(hot, logits, -jnp.inf), axis=0, keepdims=True)
        weight = jnp.where(hot, jnp.exp(jnp.where(hot, logits - top, 0.0)), 0.0)
        gate_prob = weight / jnp.sum(weight, axis=0, keepdims=True)
        arrived = to_experts(dot(picks_mat, normed_ffn).astype(jnp.bfloat16))
        gate_pre = dot(arrived, gate_mat)
        up_pre = dot(arrived, up_mat)
        hidden = (jax.nn.silu(gate_pre) * up_pre).astype(jnp.bfloat16)
        result = contract_cols(hidden, down_mat).astype(jnp.bfloat16)
        returned = from_experts(result)
        gate_rows = jnp.where(picks, gate_prob[:, None, :], 0.0).reshape(E * CAP, local_tokens)
        gate_high, gate_low = halves(gate_rows)
        saved.append(
            (
                stream,
                scale_first,
                normed_block,
                queries,
                keys_all,
                attended,
                log_total,
                middle,
                scale_second,
                normed_ffn,
                gate_prob,
                gate_rows,
                returned,
                arrived,
                gate_pre,
                up_pre,
                hidden,
                (qkv_mat, router, gain_first, gain_second, out_mat, gate_mat, up_mat, down_mat),
            )
        )
        stream = middle + contract_rows(gate_high, returned) + contract_rows(gate_low, returned)
    grad_stream = cotangent.astype(jnp.float32)
    layer_grads = [None] * LAYERS
    for layer_index in range(LAYERS - 1, -1, -1):
        (
            stream_in,
            scale_first,
            normed_block,
            queries,
            keys_all,
            attended,
            log_total,
            middle,
            scale_second,
            normed_ffn,
            gate_prob,
            gate_rows,
            returned,
            arrived,
            gate_pre,
            up_pre,
            hidden,
            (qkv_mat, router, gain_first, gain_second, out_mat, gate_mat, up_mat, down_mat),
        ) = saved[layer_index]
        grad_high, grad_low = halves(grad_stream)
        spread = dot(picks_mat, grad_high) + dot(picks_mat, grad_low)
        row_gate = jnp.sum(gate_rows, axis=1, keepdims=True)
        grad_result = to_experts((spread * row_gate).astype(jnp.bfloat16))
        row_choice = contract_cols(returned, grad_high) + contract_cols(returned, grad_low)
        grad_choice = jnp.sum(
            jnp.where(picks, row_choice.reshape(E, CAP, local_tokens), 0.0), axis=1
        )
        grad_hidden = dot(grad_result, down_mat)
        gate_sig = jax.nn.sigmoid(gate_pre)
        grad_gate_pre = (
            grad_hidden * up_pre * gate_sig * (1.0 + gate_pre * (1.0 - gate_sig))
        ).astype(jnp.bfloat16)
        grad_up_pre = (grad_hidden * gate_pre * gate_sig).astype(jnp.bfloat16)
        grad_arrived = (
            contract_cols(grad_gate_pre, gate_mat) + contract_cols(grad_up_pre, up_mat)
        ).astype(jnp.bfloat16)
        grad_rows = from_experts(grad_arrived)
        expert_grads = scatter_experts(
            [
                contract_rows(arrived, grad_gate_pre),
                contract_rows(arrived, grad_up_pre),
                contract_rows(grad_result, hidden),
            ]
        )
        grad_normed = contract_rows(picks_mat, grad_rows)
        grad_logits = gate_prob * (
            grad_choice - jnp.sum(gate_prob * grad_choice, axis=0, keepdims=True)
        )
        grad_normed = grad_normed + lax.dot_general(
            grad_logits,
            router.astype(jnp.float32),
            (((0,), (1,)), ((), ())),
            precision=PRECISE,
        )
        grad_router = lax.dot_general(
            normed_ffn.astype(jnp.float32),
            grad_logits,
            (((0,), (1,)), ((), ())),
            precision=PRECISE,
        )
        grad_middle, grad_gain_second = norm_back(middle, scale_second, gain_second, grad_normed)
        grad_stream = grad_stream + grad_middle
        branch_block = lax.all_gather(
            grad_stream.astype(jnp.bfloat16), "head", axis=0, tiled=True
        )
        grad_out = contract_rows(attended, branch_block)
        grad_attended = contract_cols(branch_block, out_mat).astype(jnp.bfloat16)
        grad_query, grad_kv = attend_back(queries, keys_all, attended, log_total, grad_attended)
        grad_query_pre = (
            rotate(
                grad_query.reshape(block_rows, H // head_count, HD).astype(jnp.float32),
                cosine_table,
                -sine_table,
            )
            .astype(jnp.bfloat16)
            .reshape(block_rows, query_cols)
        )
        grad_key_pre = (
            rotate(
                grad_kv[:, :key_cols].reshape(block_rows, key_heads, HD).astype(jnp.float32),
                cosine_table,
                -sine_table,
            )
            .astype(jnp.bfloat16)
            .reshape(block_rows, key_cols)
        )
        grad_qkv = jnp.concatenate([grad_query_pre, grad_key_pre, grad_kv[:, key_cols:]], axis=1)
        grad_normed = sum_over_head(contract_cols(grad_qkv, qkv_mat))
        grad_first, grad_gain_first = norm_back(stream_in, scale_first, gain_first, grad_normed)
        grad_stream = grad_stream + grad_first
        grad_side = jnp.concatenate(
            [grad_router, grad_gain_first[:, None], grad_gain_second[:, None]], axis=1
        )
        grad_side = jnp.pad(grad_side, ((0, 0), (0, SIDE - grad_side.shape[1])))
        grad_mats = jnp.concatenate(
            [contract_rows(normed_block, grad_qkv), grad_side], axis=1
        ).astype(jnp.bfloat16)
        grad_mats = jnp.transpose(
            grad_mats.reshape(head_count, cycle_count, shard_rows, qkv_cols + SIDE), (1, 0, 2, 3)
        )
        grad_mats = lax.all_to_all(grad_mats, "blk", split_axis=0, concat_axis=0, tiled=True)
        grad_mats = jnp.sum(grad_mats.astype(jnp.float32), axis=0).astype(jnp.bfloat16)
        grad_mats = lax.all_to_all(grad_mats, "head", split_axis=0, concat_axis=0, tiled=True)
        grad_mats = grad_mats.astype(jnp.float32)
        grad_out = lax.all_to_all(
            grad_out.astype(jnp.bfloat16).reshape(cycle_count, shard_rows, D),
            "blk",
            split_axis=0,
            concat_axis=0,
            tiled=True,
        )
        grad_out = jnp.sum(grad_out.astype(jnp.float32), axis=0)

        def joined(start, stop):
            return jnp.transpose(grad_mats[:, :, start:stop], (1, 0, 2)).reshape(shard_rows, -1)

        grad_side = jnp.sum(grad_mats[:, :, qkv_cols:], axis=0)
        layer_grads[layer_index] = (
            joined(0, query_cols),
            joined(query_cols, query_cols + key_cols),
            joined(query_cols + key_cols, qkv_cols),
            grad_out,
            grad_side[:, :E],
            grad_side[:, E],
            grad_side[:, E + 1],
        ) + expert_grads
    stacked = [
        jnp.stack([layer_grads[layer_index][member] for layer_index in range(LAYERS)])
        for member in range(10)
    ]
    return (stream, grad_stream, *stacked)


def solution(mesh):
    return jax.shard_map(
        per_device,
        mesh=mesh,
        in_specs=(
            P(("blk", "head"), None),
            P(),
            P(("blk", "head"), None),
            P(None, ("head", "blk"), None),
            P(None, ("head", "blk"), None),
            P(None, ("head", "blk"), None),
            P(None, ("head", "blk"), None),
            P(None, ("head", "blk"), None),
            P(None, ("head", "blk")),
            P(None, ("head", "blk")),
            P(None, "head", "blk", None),
            P(None, "head", "blk", None),
            P(None, "head", "blk", None),
            P(("blk", "head"), None),
        ),
        out_specs=(
            P(("blk", "head"), None),
            P(("blk", "head"), None),
            P(None, ("head", "blk"), None),
            P(None, ("head", "blk"), None),
            P(None, ("head", "blk"), None),
            P(None, ("head", "blk"), None),
            P(None, ("head", "blk"), None),
            P(None, ("head", "blk")),
            P(None, ("head", "blk")),
            P(None, "head", "blk", None),
            P(None, "head", "blk", None),
            P(None, "head", "blk", None),
        ),
        check_vma=False,
    )
```

```python
import jax
import jax.numpy as jnp
from jax import lax
from jax.sharding import PartitionSpec as P

D = 1024
H = 16
KVH = 8
HD = 64
E = 32
LAYERS = 2
CAP = 40
SIDE = 128


EPSILON = 1e-06
MASKED = -1e30
ROPE_BASE = 10000.0
PRECISE = lax.Precision.HIGHEST
BOTH = ("head", "blk")


def rms_scale(values):
    return lax.rsqrt(jnp.mean(values * values, axis=-1, keepdims=True) + EPSILON)


def rotate(values, cosine_table, sine_table):
    half_dim = values.shape[-1] // 2
    first = values[..., :half_dim]
    second = values[..., half_dim:]
    return jnp.concatenate(
        [first * cosine_table - second * sine_table, second * cosine_table + first * sine_table],
        axis=-1,
    )


def rotary_tables(start, count, head_dim):
    half_dim = head_dim // 2
    frequency = jnp.power(ROPE_BASE, -(jnp.arange(half_dim, dtype=jnp.float32) * 2.0 / head_dim))
    places = start + jnp.arange(count, dtype=jnp.int32)
    angles = places.astype(jnp.float32)[:, None] * frequency[None, :]
    return (jnp.cos(angles)[:, None, :], jnp.sin(angles)[:, None, :])


def dot(left, right):
    return jnp.dot(left, right, preferred_element_type=jnp.float32)


def contract_rows(left, right, precision=None):
    return lax.dot_general(
        left,
        right,
        (((0,), (0,)), ((), ())),
        preferred_element_type=jnp.float32,
        precision=precision,
    )


def contract_cols(left, right, precision=None):
    return lax.dot_general(
        left,
        right,
        (((1,), (1,)), ((), ())),
        preferred_element_type=jnp.float32,
        precision=precision,
    )


def halves(values):
    high = lax.reduce_precision(values, 8, 7)
    return (high.astype(jnp.bfloat16), (values - high).astype(jnp.bfloat16))


def norm_back(stream, scale, gain, grad_normed):
    inner = grad_normed * gain
    grad_gain = jnp.sum(grad_normed * stream * scale, axis=0)
    grad_stream = scale * inner - stream * scale * scale * scale * jnp.mean(
        stream * inner, axis=-1, keepdims=True
    )
    return (grad_stream, grad_gain)


def per_device(
    tokens,
    segments,
    routes,
    w_query,
    w_key,
    w_value,
    w_out,
    w_router,
    gain_attn,
    gain_ffn,
    w_gate,
    w_up,
    w_down,
    cotangent,
):
    head_count = lax.axis_size("head")
    cycle_count = lax.axis_size("blk")
    cycle_index = lax.axis_index("blk")
    local_tokens = tokens.shape[0]
    block_rows = local_tokens * head_count
    query_start = cycle_index * block_rows
    groups = H // KVH
    key_heads = KVH // head_count
    query_cols = H * HD // head_count
    key_cols = KVH * HD // head_count
    qkv_cols = query_cols + 2 * key_cols
    local_experts = E // head_count
    copies = cycle_count // local_experts
    copy_index = cycle_index % copies
    shard_rows = w_query.shape[1]
    slice_rows = w_gate.shape[2]
    hidden_units = w_gate.shape[3]
    score_scale = HD ** (-0.5)
    cosine_table, sine_table = rotary_tables(query_start, block_rows, HD)
    query_segs = lax.dynamic_slice_in_dim(segments, query_start, block_rows)
    query_pos = query_start + jnp.arange(block_rows, dtype=jnp.int32)
    block_last = segments.reshape(cycle_count, block_rows)[:, block_rows - 1]
    first_owner = jnp.sum(
        (block_last < query_segs[0]) & (jnp.arange(cycle_count) < cycle_index)
    ).astype(jnp.int32)

    hot = jnp.any(
        routes.T[None, :, :] == jnp.arange(E, dtype=jnp.int32)[:, None, None], axis=1
    )
    earlier = jnp.triu(jnp.ones((local_tokens, local_tokens), jnp.bfloat16), 1)
    slot = dot(hot.astype(jnp.bfloat16), earlier).astype(jnp.int32)
    picks = hot[:, None, :] & (
        slot[:, None, :] == jnp.arange(CAP, dtype=jnp.int32)[None, :, None]
    )
    picks_mat = picks.astype(jnp.bfloat16).reshape(E * CAP, local_tokens)

    def to_experts(rows):
        if copies > 1:
            mine = jnp.arange(copies)[None, :, None, None] == copy_index
            rows = jnp.where(mine, rows.reshape(E, 1, CAP, D), jnp.zeros((), rows.dtype))
            rows = rows.reshape(E * copies * CAP, D)
        return lax.all_to_all(rows, BOTH, split_axis=0, concat_axis=0, tiled=True)

    def from_experts(rows):
        rows = lax.all_to_all(rows, BOTH, split_axis=0, concat_axis=0, tiled=True)
        if copies > 1:
            rows = lax.dynamic_index_in_dim(
                rows.reshape(E, copies, CAP, D), copy_index, 1, keepdims=False
            ).reshape(E * CAP, D)
        return rows

    def by_head(values, cols):
        return values.reshape(LAYERS, shard_rows, head_count, cols)

    side = jnp.concatenate([w_router, gain_attn[..., None], gain_ffn[..., None]], axis=-1)
    side = jnp.pad(side, ((0, 0), (0, 0), (0, SIDE - side.shape[-1])))
    side = jnp.broadcast_to(side[:, :, None, :], (LAYERS, shard_rows, head_count, SIDE))
    sent = jnp.concatenate(
        [
            by_head(w_query, query_cols),
            by_head(w_key, key_cols),
            by_head(w_value, key_cols),
            side,
        ],
        axis=-1,
    )
    sent = jnp.transpose(sent, (2, 0, 1, 3))
    sent = lax.all_to_all(sent, "head", split_axis=0, concat_axis=0, tiled=True)
    attn_all = []
    for layer_index in range(LAYERS):
        mats = lax.all_gather(sent[:, layer_index], "blk", axis=0, tiled=False)
        attn_all.append(jnp.transpose(mats, (1, 0, 2, 3)).reshape(D, qkv_cols + SIDE))
    out_all = lax.all_gather(w_out, "blk", axis=1, tiled=True)
    tokens_block = lax.all_gather(tokens, "head", axis=0, tiled=True).astype(jnp.float32)

    def exchange_experts(layer_index):
        mats = jnp.stack([w_gate[layer_index], w_up[layer_index], w_down[layer_index]], axis=1)
        mats = jnp.repeat(mats, copies, axis=0)
        return lax.all_to_all(mats, "blk", split_axis=0, concat_axis=0, tiled=True)

    def expert_parts(mats):
        mats = jnp.transpose(mats, (1, 0, 2, 3)).reshape(3, D, hidden_units)
        return (mats[0], mats[1], mats[2])

    def exchange_grads(grads):
        grads = jnp.stack(grads).astype(jnp.bfloat16)
        grads = grads.reshape(3, cycle_count, slice_rows, hidden_units)
        grads = jnp.transpose(grads, (1, 0, 2, 3))
        return lax.all_to_all(grads, "blk", split_axis=0, concat_axis=0, tiled=True)

    def grad_parts(grads):
        grads = grads.reshape(local_experts, copies, 3, slice_rows, hidden_units)
        grads = jnp.sum(grads.astype(jnp.float32), axis=1)
        return (grads[:, 0], grads[:, 1], grads[:, 2])

    def sum_over_head(partial):
        parts = lax.all_to_all(
            partial.astype(jnp.bfloat16), "head", split_axis=0, concat_axis=0, tiled=True
        ).reshape(head_count, local_tokens, D)
        return jnp.sum(parts.astype(jnp.float32), axis=0)

    def block_mask(key_owner):
        key_start = key_owner * block_rows
        key_segs = lax.dynamic_slice_in_dim(segments, key_start, block_rows)
        key_pos = key_start + jnp.arange(block_rows, dtype=jnp.int32)
        return (query_segs[:, None] == key_segs[None, :]) & (
            query_pos[:, None] >= key_pos[None, :]
        )

    def key_block(keys_all, key_owner):
        chosen_rows = lax.dynamic_slice_in_dim(keys_all, key_owner * block_rows, block_rows)
        return (
            chosen_rows[:, :key_cols].reshape(block_rows, key_heads, HD),
            chosen_rows[:, key_cols:].reshape(block_rows, key_heads, HD),
        )

    def block_scores(query_four, key_part, allowed):
        scores = (
            jnp.einsum("qcgd,kcd->cgqk", query_four, key_part, preferred_element_type=jnp.float32)
            * score_scale
        )
        return jnp.where(allowed, scores, MASKED)

    def attend(queries, keys_all):
        query_four = queries.reshape(block_rows, key_heads, groups, HD)

        def visit(key_owner, state_in):
            running_max, running_sum, weighted = state_in
            allowed = block_mask(key_owner)
            key_part, value_part = key_block(keys_all, key_owner)
            scores = block_scores(query_four, key_part, allowed)
            new_max = jnp.maximum(running_max, jnp.max(scores, axis=-1))
            exponent = jnp.where(allowed, jnp.exp(scores - new_max[..., None]), 0.0)
            factor = jnp.exp(running_max - new_max)
            running_sum = running_sum * factor + jnp.sum(exponent, axis=-1)
            weighted = weighted * jnp.transpose(factor, (2, 0, 1))[..., None] + jnp.einsum(
                "cgqk,kcd->qcgd",
                exponent.astype(jnp.bfloat16),
                value_part,
                preferred_element_type=jnp.float32,
            )
            return (new_max, running_sum, weighted)

        start_state = (
            jnp.full((key_heads, groups, block_rows), MASKED, jnp.float32),
            jnp.zeros((key_heads, groups, block_rows), jnp.float32),
            jnp.zeros((block_rows, key_heads, groups, HD), jnp.float32),
        )
        running_max, running_sum, weighted = lax.fori_loop(
            first_owner, cycle_index + 1, visit, start_state
        )
        attended = (
            (weighted / jnp.transpose(running_sum, (2, 0, 1))[..., None])
            .astype(jnp.bfloat16)
            .reshape(block_rows, query_cols)
        )
        return (attended, running_max + jnp.log(running_sum))

    def attend_back(queries, keys_all, attended, log_total, grad_attended, beside):
        query_four = queries.reshape(block_rows, key_heads, groups, HD)
        grad_four = grad_attended.reshape(block_rows, key_heads, groups, HD)
        row_delta = jnp.transpose(
            jnp.sum(
                grad_four.astype(jnp.float32)
                * attended.reshape(block_rows, key_heads, groups, HD).astype(jnp.float32),
                axis=-1,
            ),
            (1, 2, 0),
        )

        def visit(key_owner, state_in):
            grad_query, key_grads = state_in
            allowed = block_mask(key_owner)
            key_part, value_part = key_block(keys_all, key_owner)
            scores = block_scores(query_four, key_part, allowed)
            probability = jnp.where(allowed, jnp.exp(scores - log_total[..., None]), 0.0)
            grad_value = jnp.einsum(
                "cgqk,qcgd->kcd",
                probability.astype(jnp.bfloat16),
                grad_four,
                preferred_element_type=jnp.float32,
            )
            grad_prob = jnp.einsum(
                "qcgd,kcd->cgqk", grad_four, value_part, preferred_element_type=jnp.float32
            )
            grad_scores = (probability * (grad_prob - row_delta[..., None])).astype(jnp.bfloat16)
            grad_query = grad_query + jnp.einsum(
                "cgqk,kcd->qcgd", grad_scores, key_part, preferred_element_type=jnp.float32
            )
            grad_key = (
                jnp.einsum(
                    "cgqk,qcgd->kcd", grad_scores, query_four, preferred_element_type=jnp.float32
                )
                * score_scale
            )
            stacked = jnp.concatenate(
                [grad_key.reshape(block_rows, key_cols), grad_value.reshape(block_rows, key_cols)],
                axis=1,
            ).astype(jnp.bfloat16)
            key_grads = lax.dynamic_update_slice_in_dim(
                key_grads, stacked, key_owner * block_rows, 0
            )
            return (grad_query, key_grads)

        start_state = (
            jnp.zeros((block_rows, key_heads, groups, HD), jnp.float32),
            jnp.zeros((cycle_count * block_rows, 2 * key_cols), jnp.bfloat16),
        )
        grad_query, key_grads = lax.fori_loop(first_owner, cycle_index + 1, visit, start_state)
        grad_query, key_grads, beside = lax.optimization_barrier((grad_query, key_grads, beside))
        key_grads = lax.all_to_all(key_grads, "blk", split_axis=0, concat_axis=0, tiled=True)
        key_grads = jnp.sum(
            key_grads.reshape(cycle_count, block_rows, 2 * key_cols).astype(jnp.float32), axis=0
        ).astype(jnp.bfloat16)
        grad_query = (grad_query * score_scale).astype(jnp.bfloat16)
        return (grad_query.reshape(block_rows, query_cols), key_grads, beside)

    stream = tokens.astype(jnp.float32)
    saved = []
    for layer_index in range(LAYERS):
        qkv_mat = attn_all[layer_index][:, :qkv_cols]
        side_all = attn_all[layer_index][:, qkv_cols:]
        router = side_all[:, :E]
        gain_first = side_all[:, E].astype(jnp.float32)
        gain_second = side_all[:, E + 1].astype(jnp.float32)
        out_mat = out_all[layer_index]
        scale_first = rms_scale(stream)
        if layer_index == 0:
            normed_block = (tokens_block * rms_scale(tokens_block) * gain_first).astype(
                jnp.bfloat16
            )
        else:
            normed_attn = (stream * scale_first * gain_first).astype(jnp.bfloat16)
            normed_block = lax.all_gather(normed_attn, "head", axis=0, tiled=True)
        qkv_pre = dot(normed_block, qkv_mat)
        query_pre = qkv_pre[:, :query_cols].reshape(block_rows, H // head_count, HD)
        key_pre = qkv_pre[:, query_cols : query_cols + key_cols].reshape(block_rows, key_heads, HD)
        queries = (
            rotate(query_pre, cosine_table, sine_table)
            .astype(jnp.bfloat16)
            .reshape(block_rows, query_cols)
        )
        key_rot = rotate(key_pre, cosine_table, sine_table).reshape(block_rows, key_cols)
        key_value = jnp.concatenate(
            [key_rot, qkv_pre[:, query_cols + key_cols :]], axis=1
        ).astype(jnp.bfloat16)
        keys_all = lax.all_gather(key_value, "blk", axis=0, tiled=True)
        attended, log_total = attend(queries, keys_all)
        attended, expert_mats = lax.optimization_barrier(
            (attended, exchange_experts(layer_index))
        )
        gate_mat, up_mat, down_mat = expert_parts(expert_mats)
        middle = stream + sum_over_head(dot(attended, out_mat))
        scale_second = rms_scale(middle)
        normed_ffn = (middle * scale_second * gain_second).astype(jnp.bfloat16)
        logits = lax.dot_general(
            router, normed_ffn, (((0,), (1,)), ((), ())), preferred_element_type=jnp.float32
        )
        top = jnp.max(jnp.where(hot, logits, -jnp.inf), axis=0, keepdims=True)
        weight = jnp.where(hot, jnp.exp(jnp.where(hot, logits - top, 0.0)), 0.0)
        gate_prob = weight / jnp.sum(weight, axis=0, keepdims=True)
        arrived = to_experts(dot(picks_mat, normed_ffn).astype(jnp.bfloat16))
        gate_pre = dot(arrived, gate_mat)
        up_pre = dot(arrived, up_mat)
        hidden = (jax.nn.silu(gate_pre) * up_pre).astype(jnp.bfloat16)
        result = contract_cols(hidden, down_mat).astype(jnp.bfloat16)
        returned = from_experts(result)
        gate_rows = jnp.where(picks, gate_prob[:, None, :], 0.0).reshape(E * CAP, local_tokens)
        gate_high, gate_low = halves(gate_rows)
        saved.append(
            (
                stream,
                scale_first,
                normed_block,
                queries,
                keys_all,
                attended,
                log_total,
                middle,
                scale_second,
                normed_ffn,
                gate_prob,
                gate_rows,
                returned,
                arrived,
                gate_pre,
                up_pre,
                hidden,
                (qkv_mat, router, gain_first, gain_second, out_mat, gate_mat, up_mat, down_mat),
            )
        )
        stream = middle + contract_rows(gate_high, returned) + contract_rows(gate_low, returned)
    grad_stream = cotangent.astype(jnp.float32)
    layer_grads = [None] * LAYERS
    mats_grads = [None] * LAYERS
    out_grads = [None] * LAYERS
    earlier_sums = ()
    for layer_index in range(LAYERS - 1, -1, -1):
        (
            stream_in,
            scale_first,
            normed_block,
            queries,
            keys_all,
            attended,
            log_total,
            middle,
            scale_second,
            normed_ffn,
            gate_prob,
            gate_rows,
            returned,
            arrived,
            gate_pre,
            up_pre,
            hidden,
            (qkv_mat, router, gain_first, gain_second, out_mat, gate_mat, up_mat, down_mat),
        ) = saved[layer_index]
        grad_high, grad_low = halves(grad_stream)
        spread = dot(picks_mat, grad_high) + dot(picks_mat, grad_low)
        row_gate = jnp.sum(gate_rows, axis=1, keepdims=True)
        grad_result = to_experts((spread * row_gate).astype(jnp.bfloat16))
        row_choice = contract_cols(returned, grad_high) + contract_cols(returned, grad_low)
        grad_choice = jnp.sum(
            jnp.where(picks, row_choice.reshape(E, CAP, local_tokens), 0.0), axis=1
        )
        grad_hidden = dot(grad_result, down_mat)
        gate_sig = jax.nn.sigmoid(gate_pre)
        grad_gate_pre = (
            grad_hidden * up_pre * gate_sig * (1.0 + gate_pre * (1.0 - gate_sig))
        ).astype(jnp.bfloat16)
        grad_up_pre = (grad_hidden * gate_pre * gate_sig).astype(jnp.bfloat16)
        grad_arrived = (
            contract_cols(grad_gate_pre, gate_mat) + contract_cols(grad_up_pre, up_mat)
        ).astype(jnp.bfloat16)
        grad_rows = from_experts(grad_arrived)
        expert_grads = exchange_grads(
            [
                contract_rows(arrived, grad_gate_pre),
                contract_rows(arrived, grad_up_pre),
                contract_rows(grad_result, hidden),
            ]
        )
        grad_normed = contract_rows(picks_mat, grad_rows)
        grad_logits = gate_prob * (
            grad_choice - jnp.sum(gate_prob * grad_choice, axis=0, keepdims=True)
        )
        grad_normed = grad_normed + lax.dot_general(
            grad_logits,
            router.astype(jnp.float32),
            (((0,), (1,)), ((), ())),
            precision=PRECISE,
        )
        grad_router = lax.dot_general(
            normed_ffn.astype(jnp.float32),
            grad_logits,
            (((0,), (1,)), ((), ())),
            precision=PRECISE,
        )
        grad_middle, grad_gain_second = norm_back(middle, scale_second, gain_second, grad_normed)
        grad_stream = grad_stream + grad_middle
        branch_block = lax.all_gather(
            grad_stream.astype(jnp.bfloat16), "head", axis=0, tiled=True
        )
        grad_out = contract_rows(attended, branch_block)
        grad_attended = contract_cols(branch_block, out_mat).astype(jnp.bfloat16)
        grad_query, grad_kv, (expert_grads, earlier_sums) = attend_back(
            queries, keys_all, attended, log_total, grad_attended, (expert_grads, earlier_sums)
        )
        if earlier_sums:
            mats_grads[layer_index + 1], out_grads[layer_index + 1] = earlier_sums
        grad_query_pre = (
            rotate(
                grad_query.reshape(block_rows, H // head_count, HD).astype(jnp.float32),
                cosine_table,
                -sine_table,
            )
            .astype(jnp.bfloat16)
            .reshape(block_rows, query_cols)
        )
        grad_key_pre = (
            rotate(
                grad_kv[:, :key_cols].reshape(block_rows, key_heads, HD).astype(jnp.float32),
                cosine_table,
                -sine_table,
            )
            .astype(jnp.bfloat16)
            .reshape(block_rows, key_cols)
        )
        grad_qkv = jnp.concatenate([grad_query_pre, grad_key_pre, grad_kv[:, key_cols:]], axis=1)
        grad_partial = contract_cols(grad_qkv, qkv_mat)
        grad_normed = sum_over_head(grad_partial)
        grad_gain_first = (
            jnp.sum(grad_partial * normed_block.astype(jnp.float32), axis=0) / gain_first
        )
        grad_first = norm_back(stream_in, scale_first, gain_first, grad_normed)[0]
        grad_stream = grad_stream + grad_first
        grad_side = jnp.concatenate(
            [grad_router, grad_gain_first[:, None], grad_gain_second[:, None]], axis=1
        )
        grad_side = jnp.pad(grad_side, ((0, 0), (0, SIDE - grad_side.shape[1])))
        grad_mats = jnp.concatenate(
            [contract_rows(normed_block, grad_qkv), grad_side], axis=1
        ).astype(jnp.bfloat16)
        grad_mats = jnp.transpose(
            grad_mats.reshape(head_count, cycle_count, shard_rows, qkv_cols + SIDE), (1, 0, 2, 3)
        ).reshape(cycle_count * head_count * shard_rows, qkv_cols + SIDE)
        grad_mats = lax.psum_scatter(grad_mats, "blk", scatter_dimension=0, tiled=True)
        grad_out = lax.psum_scatter(
            grad_out.astype(jnp.bfloat16), "blk", scatter_dimension=0, tiled=True
        )
        earlier_sums = (grad_mats, grad_out)
        layer_grads[layer_index] = grad_parts(expert_grads)
    mats_grads[0], out_grads[0] = earlier_sums
    mats_grads = jnp.stack(
        [sums.reshape(head_count, shard_rows, qkv_cols + SIDE) for sums in mats_grads], axis=1
    )
    mats_grads = lax.all_to_all(
        mats_grads, "head", split_axis=0, concat_axis=0, tiled=True
    ).astype(jnp.float32)

    def joined(start, stop):
        return jnp.transpose(mats_grads[..., start:stop], (1, 2, 0, 3)).reshape(
            LAYERS, shard_rows, -1
        )

    grad_side = jnp.sum(mats_grads[..., qkv_cols:], axis=0)
    gate_grads, up_grads, down_grads = [
        jnp.stack([layer_grads[layer_index][member] for layer_index in range(LAYERS)])
        for member in range(3)
    ]
    return (
        stream,
        grad_stream,
        joined(0, query_cols),
        joined(query_cols, query_cols + key_cols),
        joined(query_cols + key_cols, qkv_cols),
        jnp.stack(out_grads).astype(jnp.float32),
        grad_side[..., :E],
        grad_side[..., E],
        grad_side[..., E + 1],
        gate_grads,
        up_grads,
        down_grads,
    )


def solution(mesh):
    return jax.shard_map(
        per_device,
        mesh=mesh,
        in_specs=(
            P(("blk", "head"), None),
            P(),
            P(("blk", "head"), None),
            P(None, ("head", "blk"), None),
            P(None, ("head", "blk"), None),
            P(None, ("head", "blk"), None),
            P(None, ("head", "blk"), None),
            P(None, ("head", "blk"), None),
            P(None, ("head", "blk")),
            P(None, ("head", "blk")),
            P(None, "head", "blk", None),
            P(None, "head", "blk", None),
            P(None, "head", "blk", None),
            P(("blk", "head"), None),
        ),
        out_specs=(
            P(("blk", "head"), None),
            P(("blk", "head"), None),
            P(None, ("head", "blk"), None),
            P(None, ("head", "blk"), None),
            P(None, ("head", "blk"), None),
            P(None, ("head", "blk"), None),
            P(None, ("head", "blk"), None),
            P(None, ("head", "blk")),
            P(None, ("head", "blk")),
            P(None, "head", "blk", None),
            P(None, "head", "blk", None),
            P(None, "head", "blk", None),
        ),
        check_vma=False,
    )
```

```python
import functools

import jax
import jax.numpy as jnp
from jax import lax
from jax.experimental import pallas as pl
from jax.experimental.pallas import tpu as pltpu
from jax.sharding import PartitionSpec as P

D = 1024
H = 16
KVH = 8
HD = 64
E = 32
LAYERS = 2
CAP = 40
SIDE = 128
LANES = 128
SUBLANES = 8


EPSILON = 1e-06
MASKED = -1e30
ROPE_BASE = 10000.0
PRECISE = lax.Precision.HIGHEST
BOTH = ("head", "blk")


def rms_scale(values):
    return lax.rsqrt(jnp.mean(values * values, axis=-1, keepdims=True) + EPSILON)


def rotate(values, cosine_table, sine_table):
    half_dim = values.shape[-1] // 2
    first = values[..., :half_dim]
    second = values[..., half_dim:]
    return jnp.concatenate(
        [first * cosine_table - second * sine_table, second * cosine_table + first * sine_table],
        axis=-1,
    )


def rotary_tables(start, count, head_dim):
    half_dim = head_dim // 2
    frequency = jnp.power(ROPE_BASE, -(jnp.arange(half_dim, dtype=jnp.float32) * 2.0 / head_dim))
    places = start + jnp.arange(count, dtype=jnp.int32)
    angles = places.astype(jnp.float32)[:, None] * frequency[None, :]
    return (jnp.cos(angles)[:, None, :], jnp.sin(angles)[:, None, :])


def dot(left, right):
    return jnp.dot(left, right, preferred_element_type=jnp.float32)


def contract_rows(left, right, precision=None):
    return lax.dot_general(
        left,
        right,
        (((0,), (0,)), ((), ())),
        preferred_element_type=jnp.float32,
        precision=precision,
    )


def contract_cols(left, right, precision=None):
    return lax.dot_general(
        left,
        right,
        (((1,), (1,)), ((), ())),
        preferred_element_type=jnp.float32,
        precision=precision,
    )


def halves(values):
    high = lax.reduce_precision(values, 8, 7)
    return (high.astype(jnp.bfloat16), (values - high).astype(jnp.bfloat16))


def lane_half(shape):
    return lax.broadcasted_iota(jnp.int32, shape, 1) // HD


def head_lanes(values, head, groups):
    tile = values[:, head // 2 * LANES : (head // 2 + 1) * LANES]
    wanted = head // groups
    if head % 2 != wanted:
        tile = pltpu.roll(tile, HD, 1)
    return jnp.where(lane_half(tile.shape) == wanted, tile, 0.0)


def attend_kernel(heads, groups, bounds, q_ref, kv_ref, start_ref, o_ref, lse_ref, high, total, acc):
    rows = q_ref.shape[0]
    scaled = q_ref[...].astype(jnp.float32) * HD ** (-0.5)
    queries = [head_lanes(scaled, head, groups).astype(jnp.bfloat16) for head in range(heads)]
    starts = start_ref[...]
    spots = bounds[2] + lax.broadcasted_iota(jnp.int32, (rows, 1), 0)
    high[...] = jnp.full(high.shape, MASKED, jnp.float32)
    total[...] = jnp.zeros(total.shape, jnp.float32)
    acc[...] = jnp.zeros(acc.shape, jnp.float32)

    @pl.loop(bounds[0], bounds[1])
    def _(owner):
        first = pl.multiple_of(owner * rows, rows)
        keys = kv_ref[pl.ds(first, rows), :LANES]
        values = kv_ref[pl.ds(first, rows), LANES:]
        places = first + lax.broadcasted_iota(jnp.int32, (rows, rows), 1)
        bias = jnp.where((places >= starts) & (places <= spots), 0.0, MASKED)
        for head in range(heads):
            scores = contract_cols(queries[head], keys) + bias
            old = high[head]
            new = jnp.maximum(old, jnp.max(scores, axis=1, keepdims=True))
            exponent = jnp.exp(scores - new)
            factor = jnp.exp(old - new)
            total[head] = total[head] * factor + jnp.sum(exponent, axis=1, keepdims=True)
            acc[head] = acc[head] * factor + dot(exponent.astype(jnp.bfloat16), values)
            high[head] = new

    lanes = lax.broadcasted_iota(jnp.int32, (rows, LANES), 1)
    logs = jnp.zeros((rows, LANES), jnp.float32)
    for pair in range(heads // 2):
        tile = jnp.zeros((rows, LANES), jnp.float32)
        for head in (2 * pair, 2 * pair + 1):
            part = acc[head] / total[head]
            if head % 2 != head // groups:
                part = pltpu.roll(part, HD, 1)
            tile = jnp.where(lane_half(part.shape) == head % 2, part, tile)
            logs = jnp.where(lanes == head, high[head] + jnp.log(total[head]), logs)
        o_ref[:, pair * LANES : (pair + 1) * LANES] = tile.astype(jnp.bfloat16)
    lse_ref[...] = logs.T[:SUBLANES]


def attend_back_kernel(
    heads,
    groups,
    bounds,
    q_ref,
    kv_ref,
    start_ref,
    o_ref,
    lse_ref,
    g_ref,
    gq_ref,
    gkv_ref,
    q_sc,
    qt_sc,
    g_sc,
    gt_sc,
    acc,
):
    rows = q_ref.shape[0]
    scaled = q_ref[...].astype(jnp.float32) * HD ** (-0.5)
    grads = g_ref[...].astype(jnp.float32)
    outs = o_ref[...].astype(jnp.float32)
    lanes = lax.broadcasted_iota(jnp.int32, (rows, LANES), 1)
    deltas = jnp.zeros((rows, LANES), jnp.float32)
    for head in range(heads):
        query = head_lanes(scaled, head, groups)
        q_sc[head] = query.astype(jnp.bfloat16)
        qt_sc[head] = query.T.astype(jnp.bfloat16)
        grad = head_lanes(grads, head, groups)
        g_sc[head] = grad.astype(jnp.bfloat16)
        gt_sc[head] = grad.T.astype(jnp.bfloat16)
        delta = jnp.sum(grad * head_lanes(outs, head, groups), axis=1, keepdims=True)
        deltas = jnp.where(lanes == head, delta, deltas)
    deltas = deltas.T
    logs = lse_ref[...]
    starts = start_ref[...]
    spots = bounds[2] + lax.broadcasted_iota(jnp.int32, (1, rows), 1)
    gkv_ref[...] = jnp.zeros(gkv_ref.shape, gkv_ref.dtype)
    acc[...] = jnp.zeros(acc.shape, jnp.float32)

    @pl.loop(bounds[0], bounds[1])
    def _(owner):
        first = pl.multiple_of(owner * rows, rows)
        keys = kv_ref[pl.ds(first, rows), :LANES]
        values = kv_ref[pl.ds(first, rows), LANES:]
        keys_turned = keys.astype(jnp.float32).T.astype(jnp.bfloat16)
        places = first + lax.broadcasted_iota(jnp.int32, (rows, rows), 0)
        bias = jnp.where((places >= starts) & (places <= spots), 0.0, MASKED)
        grad_keys = jnp.zeros((rows, LANES), jnp.float32)
        grad_values = jnp.zeros((rows, LANES), jnp.float32)
        for head in range(heads):
            wanted = head // groups
            scores = dot(keys, qt_sc[head]) + bias
            probability = jnp.exp(scores - logs[head : head + 1])
            grad_values += dot(probability.astype(jnp.bfloat16), g_sc[head])
            grad_prob = dot(values, gt_sc[head])
            grad_scores = (probability * (grad_prob - deltas[head : head + 1])).astype(
                jnp.bfloat16
            )
            grad_keys += dot(grad_scores, q_sc[head])
            acc[head * HD : (head + 1) * HD] += dot(
                keys_turned[wanted * HD : (wanted + 1) * HD], grad_scores
            )
        gkv_ref[pl.ds(first, rows), :LANES] = grad_keys.astype(jnp.bfloat16)
        gkv_ref[pl.ds(first, rows), LANES:] = grad_values.astype(jnp.bfloat16)

    gq_ref[...] = (acc[...].T * HD ** (-0.5)).astype(jnp.bfloat16)


def norm_back(stream, scale, gain, grad_normed):
    inner = grad_normed * gain
    grad_gain = jnp.sum(grad_normed * stream * scale, axis=0)
    grad_stream = scale * inner - stream * scale * scale * scale * jnp.mean(
        stream * inner, axis=-1, keepdims=True
    )
    return (grad_stream, grad_gain)


def per_device(
    tokens,
    segments,
    routes,
    w_query,
    w_key,
    w_value,
    w_out,
    w_router,
    gain_attn,
    gain_ffn,
    w_gate,
    w_up,
    w_down,
    cotangent,
):
    head_count = lax.axis_size("head")
    cycle_count = lax.axis_size("blk")
    cycle_index = lax.axis_index("blk")
    local_tokens = tokens.shape[0]
    block_rows = local_tokens * head_count
    query_start = cycle_index * block_rows
    groups = H // KVH
    key_heads = KVH // head_count
    query_cols = H * HD // head_count
    key_cols = KVH * HD // head_count
    qkv_cols = query_cols + 2 * key_cols
    local_experts = E // head_count
    copies = cycle_count // local_experts
    copy_index = cycle_index % copies
    shard_rows = w_query.shape[1]
    slice_rows = w_gate.shape[2]
    hidden_units = w_gate.shape[3]
    score_scale = HD ** (-0.5)
    cosine_table, sine_table = rotary_tables(query_start, block_rows, HD)
    query_segs = lax.dynamic_slice_in_dim(segments, query_start, block_rows)
    block_last = segments.reshape(cycle_count, block_rows)[:, block_rows - 1]
    first_owner = jnp.sum(
        (block_last < query_segs[0]) & (jnp.arange(cycle_count) < cycle_index)
    ).astype(jnp.int32)

    hot = jnp.any(
        routes.T[None, :, :] == jnp.arange(E, dtype=jnp.int32)[:, None, None], axis=1
    )
    earlier = jnp.triu(jnp.ones((local_tokens, local_tokens), jnp.bfloat16), 1)
    slot = dot(hot.astype(jnp.bfloat16), earlier).astype(jnp.int32)
    picks = hot[:, None, :] & (
        slot[:, None, :] == jnp.arange(CAP, dtype=jnp.int32)[None, :, None]
    )
    picks_mat = picks.astype(jnp.bfloat16).reshape(E * CAP, local_tokens)

    def to_experts(rows):
        if copies > 1:
            mine = jnp.arange(copies)[None, :, None, None] == copy_index
            rows = jnp.where(mine, rows.reshape(E, 1, CAP, D), jnp.zeros((), rows.dtype))
            rows = rows.reshape(E * copies * CAP, D)
        return lax.all_to_all(rows, BOTH, split_axis=0, concat_axis=0, tiled=True)

    def from_experts(rows):
        rows = lax.all_to_all(rows, BOTH, split_axis=0, concat_axis=0, tiled=True)
        if copies > 1:
            rows = lax.dynamic_index_in_dim(
                rows.reshape(E, copies, CAP, D), copy_index, 1, keepdims=False
            ).reshape(E * CAP, D)
        return rows

    def by_head(values, cols):
        return values.reshape(LAYERS, shard_rows, head_count, cols)

    side = jnp.concatenate([w_router, gain_attn[..., None], gain_ffn[..., None]], axis=-1)
    side = jnp.pad(side, ((0, 0), (0, 0), (0, SIDE - side.shape[-1])))
    side = jnp.broadcast_to(side[:, :, None, :], (LAYERS, shard_rows, head_count, SIDE))
    sent = jnp.concatenate(
        [
            by_head(w_query, query_cols),
            by_head(w_key, key_cols),
            by_head(w_value, key_cols),
            side,
        ],
        axis=-1,
    )
    sent = jnp.transpose(sent, (2, 0, 1, 3))
    sent = lax.all_to_all(sent, "head", split_axis=0, concat_axis=0, tiled=True)
    attn_all = []
    for layer_index in range(LAYERS):
        mats = lax.all_gather(sent[:, layer_index], "blk", axis=0, tiled=False)
        attn_all.append(jnp.transpose(mats, (1, 0, 2, 3)).reshape(D, qkv_cols + SIDE))
    tokens_block = lax.all_gather(tokens, "head", axis=0, tiled=True).astype(jnp.float32)

    def exchange_experts(layer_index):
        mats = jnp.stack([w_gate[layer_index], w_up[layer_index], w_down[layer_index]], axis=1)
        mats = jnp.repeat(mats, copies, axis=0)
        return lax.all_to_all(mats, "blk", split_axis=0, concat_axis=0, tiled=True)

    def expert_parts(mats):
        mats = jnp.transpose(mats, (1, 0, 2, 3)).reshape(3, D, hidden_units)
        return (mats[0], mats[1], mats[2])

    def exchange_grads(grads):
        grads = jnp.stack(grads).astype(jnp.bfloat16)
        grads = grads.reshape(3, cycle_count, slice_rows, hidden_units)
        grads = jnp.transpose(grads, (1, 0, 2, 3))
        return lax.all_to_all(grads, "blk", split_axis=0, concat_axis=0, tiled=True)

    def grad_parts(grads):
        grads = grads.reshape(local_experts, copies, 3, slice_rows, hidden_units)
        grads = jnp.sum(grads.astype(jnp.float32), axis=1)
        return (grads[:, 0], grads[:, 1], grads[:, 2])

    def sum_over_head(partial):
        parts = lax.all_to_all(
            partial.astype(jnp.bfloat16), "head", split_axis=0, concat_axis=0, tiled=True
        ).reshape(head_count, local_tokens, D)
        return jnp.sum(parts.astype(jnp.float32), axis=0)

    local_heads = H // head_count
    bounds = jnp.stack([first_owner, cycle_index + 1, query_start]).astype(jnp.int32)
    starts = jnp.sum(
        (segments[None, :] < query_segs[:, None]).astype(jnp.int32), axis=1, dtype=jnp.int32
    )
    in_smem = pl.BlockSpec(memory_space=pltpu.SMEM)
    in_vmem = pl.BlockSpec(memory_space=pltpu.VMEM)

    def widen(keys_all):
        parts = keys_all.reshape(-1, 2, key_cols)
        parts = jnp.pad(parts, ((0, 0), (0, 0), (0, LANES - key_cols)))
        return parts.reshape(-1, 2 * LANES)

    def narrow(key_grads):
        return key_grads.reshape(-1, 2, LANES)[:, :, :key_cols].reshape(-1, 2 * key_cols)

    def attend(queries, keys_wide):
        total_rows = keys_wide.shape[0]
        return pl.pallas_call(
            functools.partial(attend_kernel, local_heads, groups),
            out_shape=(
                jax.ShapeDtypeStruct((block_rows, query_cols), jnp.bfloat16),
                jax.ShapeDtypeStruct((SUBLANES, block_rows), jnp.float32),
            ),
            in_specs=[in_smem, in_vmem, in_vmem, in_vmem],
            out_specs=(in_vmem, in_vmem),
            scratch_shapes=[
                pltpu.VMEM((local_heads, block_rows, 1), jnp.float32),
                pltpu.VMEM((local_heads, block_rows, 1), jnp.float32),
                pltpu.VMEM((local_heads, block_rows, LANES), jnp.float32),
            ],
            cost_estimate=pl.CostEstimate(
                flops=2 * block_rows * total_rows * LANES * local_heads,
                bytes_accessed=2 * total_rows * 2 * LANES,
                transcendentals=block_rows * total_rows * local_heads,
            ),
            name="attend",
        )(bounds, queries, keys_wide, starts[:, None])

    def attend_back(queries, keys_wide, attended, log_total, grad_attended, beside):
        total_rows = keys_wide.shape[0]
        scratch = [pltpu.VMEM((local_heads, block_rows, LANES), jnp.bfloat16)]
        turned = [pltpu.VMEM((local_heads, LANES, block_rows), jnp.bfloat16)]
        grad_query, key_grads = pl.pallas_call(
            functools.partial(attend_back_kernel, local_heads, groups),
            out_shape=(
                jax.ShapeDtypeStruct((block_rows, query_cols), jnp.bfloat16),
                jax.ShapeDtypeStruct((total_rows, 2 * LANES), jnp.bfloat16),
            ),
            in_specs=[in_smem] + [in_vmem] * 6,
            out_specs=(in_vmem, in_vmem),
            scratch_shapes=(scratch + turned) * 2
            + [pltpu.VMEM((query_cols, block_rows), jnp.float32)],
            cost_estimate=pl.CostEstimate(
                flops=5 * block_rows * total_rows * LANES * local_heads,
                bytes_accessed=4 * total_rows * 2 * LANES,
                transcendentals=block_rows * total_rows * local_heads,
            ),
            name="attend_back",
        )(bounds, queries, keys_wide, starts[None, :], attended, log_total, grad_attended)
        grad_query, key_grads, beside = lax.optimization_barrier((grad_query, key_grads, beside))
        key_grads = lax.all_to_all(
            narrow(key_grads), "blk", split_axis=0, concat_axis=0, tiled=True
        )
        key_grads = jnp.sum(
            key_grads.reshape(cycle_count, block_rows, 2 * key_cols).astype(jnp.float32), axis=0
        ).astype(jnp.bfloat16)
        return (grad_query, key_grads, beside)

    stream = tokens.astype(jnp.float32)
    saved = []
    for layer_index in range(LAYERS):
        qkv_mat = attn_all[layer_index][:, :qkv_cols]
        side_all = attn_all[layer_index][:, qkv_cols:]
        router = side_all[:, :E]
        gain_first = side_all[:, E].astype(jnp.float32)
        gain_second = side_all[:, E + 1].astype(jnp.float32)
        out_mat = lax.all_gather(w_out[layer_index], BOTH, axis=0, tiled=True)
        scale_first = rms_scale(stream)
        if layer_index == 0:
            normed_block = (tokens_block * rms_scale(tokens_block) * gain_first).astype(
                jnp.bfloat16
            )
        else:
            normed_attn = (stream * scale_first * gain_first).astype(jnp.bfloat16)
            normed_block = lax.all_gather(normed_attn, "head", axis=0, tiled=True)
        qkv_pre = dot(normed_block, qkv_mat)
        query_pre = qkv_pre[:, :query_cols].reshape(block_rows, H // head_count, HD)
        key_pre = qkv_pre[:, query_cols : query_cols + key_cols].reshape(block_rows, key_heads, HD)
        queries = (
            rotate(query_pre, cosine_table, sine_table)
            .astype(jnp.bfloat16)
            .reshape(block_rows, query_cols)
        )
        key_rot = rotate(key_pre, cosine_table, sine_table).reshape(block_rows, key_cols)
        key_value = jnp.concatenate(
            [key_rot, qkv_pre[:, query_cols + key_cols :]], axis=1
        ).astype(jnp.bfloat16)
        keys_all = widen(lax.all_gather(key_value, "blk", axis=0, tiled=True))
        attended, log_total = attend(queries, keys_all)
        attended, expert_mats = lax.optimization_barrier(
            (attended, exchange_experts(layer_index))
        )
        gate_mat, up_mat, down_mat = expert_parts(expert_mats)
        attended_tok = lax.all_to_all(attended, "head", split_axis=0, concat_axis=1, tiled=True)
        middle = stream + dot(attended_tok, out_mat)
        scale_second = rms_scale(middle)
        normed_ffn = (middle * scale_second * gain_second).astype(jnp.bfloat16)
        logits = lax.dot_general(
            router, normed_ffn, (((0,), (1,)), ((), ())), preferred_element_type=jnp.float32
        )
        top = jnp.max(jnp.where(hot, logits, -jnp.inf), axis=0, keepdims=True)
        weight = jnp.where(hot, jnp.exp(jnp.where(hot, logits - top, 0.0)), 0.0)
        gate_prob = weight / jnp.sum(weight, axis=0, keepdims=True)
        arrived = to_experts(dot(picks_mat, normed_ffn).astype(jnp.bfloat16))
        gate_pre = dot(arrived, gate_mat)
        up_pre = dot(arrived, up_mat)
        hidden = (jax.nn.silu(gate_pre) * up_pre).astype(jnp.bfloat16)
        result = contract_cols(hidden, down_mat).astype(jnp.bfloat16)
        returned = from_experts(result)
        gate_rows = jnp.where(picks, gate_prob[:, None, :], 0.0).reshape(E * CAP, local_tokens)
        gate_high, gate_low = halves(gate_rows)
        saved.append(
            (
                stream,
                scale_first,
                normed_block,
                queries,
                keys_all,
                attended,
                attended_tok,
                log_total,
                middle,
                scale_second,
                normed_ffn,
                gate_prob,
                gate_rows,
                returned,
                arrived,
                gate_pre,
                up_pre,
                hidden,
                (qkv_mat, router, gain_first, gain_second, out_mat, gate_mat, up_mat, down_mat),
            )
        )
        stream = middle + contract_rows(gate_high, returned) + contract_rows(gate_low, returned)
    grad_stream = cotangent.astype(jnp.float32)
    layer_grads = [None] * LAYERS
    mats_grads = [None] * LAYERS
    out_grads = [None] * LAYERS
    earlier_sums = ()
    for layer_index in range(LAYERS - 1, -1, -1):
        (
            stream_in,
            scale_first,
            normed_block,
            queries,
            keys_all,
            attended,
            attended_tok,
            log_total,
            middle,
            scale_second,
            normed_ffn,
            gate_prob,
            gate_rows,
            returned,
            arrived,
            gate_pre,
            up_pre,
            hidden,
            (qkv_mat, router, gain_first, gain_second, out_mat, gate_mat, up_mat, down_mat),
        ) = saved[layer_index]
        grad_high, grad_low = halves(grad_stream)
        spread = dot(picks_mat, grad_high) + dot(picks_mat, grad_low)
        row_gate = jnp.sum(gate_rows, axis=1, keepdims=True)
        grad_result = to_experts((spread * row_gate).astype(jnp.bfloat16))
        row_choice = contract_cols(returned, grad_high) + contract_cols(returned, grad_low)
        grad_choice = jnp.sum(
            jnp.where(picks, row_choice.reshape(E, CAP, local_tokens), 0.0), axis=1
        )
        grad_hidden = dot(grad_result, down_mat)
        gate_sig = jax.nn.sigmoid(gate_pre)
        grad_gate_pre = (
            grad_hidden * up_pre * gate_sig * (1.0 + gate_pre * (1.0 - gate_sig))
        ).astype(jnp.bfloat16)
        grad_up_pre = (grad_hidden * gate_pre * gate_sig).astype(jnp.bfloat16)
        grad_arrived = (
            contract_cols(grad_gate_pre, gate_mat) + contract_cols(grad_up_pre, up_mat)
        ).astype(jnp.bfloat16)
        grad_rows = from_experts(grad_arrived)
        expert_grads = exchange_grads(
            [
                contract_rows(arrived, grad_gate_pre),
                contract_rows(arrived, grad_up_pre),
                contract_rows(grad_result, hidden),
            ]
        )
        grad_normed = contract_rows(picks_mat, grad_rows)
        grad_logits = gate_prob * (
            grad_choice - jnp.sum(gate_prob * grad_choice, axis=0, keepdims=True)
        )
        grad_normed = grad_normed + lax.dot_general(
            grad_logits,
            router.astype(jnp.float32),
            (((0,), (1,)), ((), ())),
            precision=PRECISE,
        )
        grad_router = lax.dot_general(
            normed_ffn.astype(jnp.float32),
            grad_logits,
            (((0,), (1,)), ((), ())),
            precision=PRECISE,
        )
        grad_middle, grad_gain_second = norm_back(middle, scale_second, gain_second, grad_normed)
        grad_stream = grad_stream + grad_middle
        grad_branch = grad_stream.astype(jnp.bfloat16)
        grad_attended = contract_cols(grad_branch, out_mat).astype(jnp.bfloat16)
        grad_attended = lax.all_to_all(
            grad_attended, "head", split_axis=1, concat_axis=0, tiled=True
        )
        grad_out = contract_rows(attended_tok, grad_branch)
        grad_query, grad_kv, (expert_grads, earlier_sums) = attend_back(
            queries, keys_all, attended, log_total, grad_attended, (expert_grads, earlier_sums)
        )
        if earlier_sums:
            mats_grads[layer_index + 1], out_grads[layer_index + 1] = earlier_sums
        grad_query_pre = (
            rotate(
                grad_query.reshape(block_rows, H // head_count, HD).astype(jnp.float32),
                cosine_table,
                -sine_table,
            )
            .astype(jnp.bfloat16)
            .reshape(block_rows, query_cols)
        )
        grad_key_pre = (
            rotate(
                grad_kv[:, :key_cols].reshape(block_rows, key_heads, HD).astype(jnp.float32),
                cosine_table,
                -sine_table,
            )
            .astype(jnp.bfloat16)
            .reshape(block_rows, key_cols)
        )
        grad_qkv = jnp.concatenate([grad_query_pre, grad_key_pre, grad_kv[:, key_cols:]], axis=1)
        grad_partial = contract_cols(grad_qkv, qkv_mat)
        grad_normed = sum_over_head(grad_partial)
        grad_gain_first = (
            jnp.sum(grad_partial * normed_block.astype(jnp.float32), axis=0) / gain_first
        )
        grad_first = norm_back(stream_in, scale_first, gain_first, grad_normed)[0]
        grad_stream = grad_stream + grad_first
        grad_side = jnp.concatenate(
            [grad_router, grad_gain_first[:, None], grad_gain_second[:, None]], axis=1
        )
        grad_side = jnp.pad(grad_side, ((0, 0), (0, SIDE - grad_side.shape[1])))
        grad_mats = jnp.concatenate(
            [contract_rows(normed_block, grad_qkv), grad_side], axis=1
        ).astype(jnp.bfloat16)
        grad_mats = jnp.transpose(
            grad_mats.reshape(head_count, cycle_count, shard_rows, qkv_cols + SIDE), (1, 0, 2, 3)
        ).reshape(cycle_count * head_count * shard_rows, qkv_cols + SIDE)
        grad_mats = lax.psum_scatter(grad_mats, "blk", scatter_dimension=0, tiled=True)
        grad_out = lax.psum_scatter(
            grad_out.astype(jnp.bfloat16), BOTH, scatter_dimension=0, tiled=True
        )
        earlier_sums = (grad_mats, grad_out)
        layer_grads[layer_index] = grad_parts(expert_grads)
    mats_grads[0], out_grads[0] = earlier_sums
    mats_grads = jnp.stack(
        [sums.reshape(head_count, shard_rows, qkv_cols + SIDE) for sums in mats_grads], axis=1
    )
    mats_grads = lax.all_to_all(
        mats_grads, "head", split_axis=0, concat_axis=0, tiled=True
    ).astype(jnp.float32)

    def joined(start, stop):
        return jnp.transpose(mats_grads[..., start:stop], (1, 2, 0, 3)).reshape(
            LAYERS, shard_rows, -1
        )

    grad_side = jnp.sum(mats_grads[..., qkv_cols:], axis=0)
    gate_grads, up_grads, down_grads = [
        jnp.stack([layer_grads[layer_index][member] for layer_index in range(LAYERS)])
        for member in range(3)
    ]
    return (
        stream,
        grad_stream,
        joined(0, query_cols),
        joined(query_cols, query_cols + key_cols),
        joined(query_cols + key_cols, qkv_cols),
        jnp.stack(out_grads).astype(jnp.float32),
        grad_side[..., :E],
        grad_side[..., E],
        grad_side[..., E + 1],
        gate_grads,
        up_grads,
        down_grads,
    )


def solution(mesh):
    return jax.shard_map(
        per_device,
        mesh=mesh,
        in_specs=(
            P(("blk", "head"), None),
            P(),
            P(("blk", "head"), None),
            P(None, ("head", "blk"), None),
            P(None, ("head", "blk"), None),
            P(None, ("head", "blk"), None),
            P(None, ("head", "blk"), None),
            P(None, ("head", "blk"), None),
            P(None, ("head", "blk")),
            P(None, ("head", "blk")),
            P(None, "head", "blk", None),
            P(None, "head", "blk", None),
            P(None, "head", "blk", None),
            P(("blk", "head"), None),
        ),
        out_specs=(
            P(("blk", "head"), None),
            P(("blk", "head"), None),
            P(None, ("head", "blk"), None),
            P(None, ("head", "blk"), None),
            P(None, ("head", "blk"), None),
            P(None, ("head", "blk"), None),
            P(None, ("head", "blk"), None),
            P(None, ("head", "blk")),
            P(None, ("head", "blk")),
            P(None, "head", "blk", None),
            P(None, "head", "blk", None),
            P(None, "head", "blk", None),
        ),
        check_vma=False,
    )
```

```python
import functools

import jax
import jax.numpy as jnp
from jax import lax
from jax.experimental import pallas as pl
from jax.experimental.pallas import tpu as pltpu
from jax.sharding import PartitionSpec as P

D = 1024
H = 16
KVH = 8
HD = 64
E = 32
LAYERS = 2
CAP = 40
SIDE = 128
LANES = 128
SUBLANES = 8


EPSILON = 1e-06
MASKED = -1e30
ROPE_BASE = 10000.0
PRECISE = lax.Precision.HIGHEST
BOTH = ("head", "blk")


def rms_scale(values):
    return lax.rsqrt(jnp.mean(values * values, axis=-1, keepdims=True) + EPSILON)


def rotate(values, cosine_table, sine_table):
    half_dim = values.shape[-1] // 2
    first = values[..., :half_dim]
    second = values[..., half_dim:]
    return jnp.concatenate(
        [first * cosine_table - second * sine_table, second * cosine_table + first * sine_table],
        axis=-1,
    )


def rotary_tables(start, count, head_dim):
    half_dim = head_dim // 2
    frequency = jnp.power(ROPE_BASE, -(jnp.arange(half_dim, dtype=jnp.float32) * 2.0 / head_dim))
    places = start + jnp.arange(count, dtype=jnp.int32)
    angles = places.astype(jnp.float32)[:, None] * frequency[None, :]
    return (jnp.cos(angles)[:, None, :], jnp.sin(angles)[:, None, :])


def dot(left, right):
    return jnp.dot(left, right, preferred_element_type=jnp.float32)


def contract_rows(left, right, precision=None):
    return lax.dot_general(
        left,
        right,
        (((0,), (0,)), ((), ())),
        preferred_element_type=jnp.float32,
        precision=precision,
    )


def contract_cols(left, right, precision=None):
    return lax.dot_general(
        left,
        right,
        (((1,), (1,)), ((), ())),
        preferred_element_type=jnp.float32,
        precision=precision,
    )


def halves(values):
    high = lax.reduce_precision(values, 8, 7)
    return (high.astype(jnp.bfloat16), (values - high).astype(jnp.bfloat16))


def lane_half(shape):
    return lax.broadcasted_iota(jnp.int32, shape, 1) // HD


def head_lanes(values, head, groups):
    tile = values[:, head // 2 * LANES : (head // 2 + 1) * LANES]
    wanted = head // groups
    if head % 2 != wanted:
        tile = pltpu.roll(tile, HD, 1)
    return jnp.where(lane_half(tile.shape) == wanted, tile, 0.0)


def attend_kernel(
    heads, groups, bounds, q_ref, kv_ref, start_ref, o_ref, lse_ref, qt_sc, high, total, acc
):
    rows = q_ref.shape[0]
    scaled = q_ref[...].astype(jnp.float32) * HD ** (-0.5)
    for head in range(heads):
        qt_sc[head] = head_lanes(scaled, head, groups).T.astype(jnp.bfloat16)
    starts = start_ref[...]
    spots = bounds[2] + lax.broadcasted_iota(jnp.int32, (1, rows), 1)
    high[...] = jnp.full(high.shape, MASKED, jnp.float32)
    total[...] = jnp.ones(total.shape, jnp.float32)
    acc[...] = jnp.zeros(acc.shape, jnp.float32)

    @pl.loop(bounds[0], bounds[1])
    def _(owner):
        first = pl.multiple_of(owner * rows, rows)
        keys = kv_ref[pl.ds(first, rows), :LANES]
        values = kv_ref[pl.ds(first, rows), LANES:].astype(jnp.float32).T.astype(jnp.bfloat16)
        places = first + lax.broadcasted_iota(jnp.int32, (rows, rows), 0)
        bias = jnp.where((places >= starts) & (places <= spots), 0.0, MASKED)
        for head in range(heads):
            wanted = head // groups
            scores = dot(keys, qt_sc[head]) + bias
            old = high[head : head + 1]
            new = jnp.maximum(old, jnp.max(scores, axis=0, keepdims=True))
            exponent = jnp.exp(scores - new)
            factor = jnp.exp(old - new)
            total[head : head + 1] = total[head : head + 1] * factor + jnp.sum(
                exponent, axis=0, keepdims=True
            )
            acc[head * HD : (head + 1) * HD] = acc[head * HD : (head + 1) * HD] * factor + dot(
                values[wanted * HD : (wanted + 1) * HD], exponent.astype(jnp.bfloat16)
            )
            high[head : head + 1] = new

    lse_ref[...] = high[...] + jnp.log(total[...])
    for head in range(heads):
        acc[head * HD : (head + 1) * HD] = (
            acc[head * HD : (head + 1) * HD] / total[head : head + 1]
        )
    o_ref[...] = acc[...].T.astype(jnp.bfloat16)


def attend_back_kernel(
    heads,
    groups,
    bounds,
    q_ref,
    kv_ref,
    start_ref,
    o_ref,
    lse_ref,
    g_ref,
    gq_ref,
    gkv_ref,
    q_sc,
    qt_sc,
    g_sc,
    gt_sc,
    acc,
):
    rows = q_ref.shape[0]
    scaled = q_ref[...].astype(jnp.float32) * HD ** (-0.5)
    grads = g_ref[...].astype(jnp.float32)
    outs = o_ref[...].astype(jnp.float32)
    lanes = lax.broadcasted_iota(jnp.int32, (rows, LANES), 1)
    deltas = jnp.zeros((rows, LANES), jnp.float32)
    for head in range(heads):
        query = head_lanes(scaled, head, groups)
        q_sc[head] = query.astype(jnp.bfloat16)
        qt_sc[head] = query.T.astype(jnp.bfloat16)
        grad = head_lanes(grads, head, groups)
        g_sc[head] = grad.astype(jnp.bfloat16)
        gt_sc[head] = grad.T.astype(jnp.bfloat16)
        delta = jnp.sum(grad * head_lanes(outs, head, groups), axis=1, keepdims=True)
        deltas = jnp.where(lanes == head, delta, deltas)
    deltas = deltas.T
    logs = lse_ref[...]
    starts = start_ref[...]
    spots = bounds[2] + lax.broadcasted_iota(jnp.int32, (1, rows), 1)
    gkv_ref[...] = jnp.zeros(gkv_ref.shape, gkv_ref.dtype)
    acc[...] = jnp.zeros(acc.shape, jnp.float32)

    @pl.loop(bounds[0], bounds[1])
    def _(owner):
        first = pl.multiple_of(owner * rows, rows)
        keys = kv_ref[pl.ds(first, rows), :LANES]
        values = kv_ref[pl.ds(first, rows), LANES:]
        keys_turned = keys.astype(jnp.float32).T.astype(jnp.bfloat16)
        places = first + lax.broadcasted_iota(jnp.int32, (rows, rows), 0)
        bias = jnp.where((places >= starts) & (places <= spots), 0.0, MASKED)
        grad_keys = jnp.zeros((rows, LANES), jnp.float32)
        grad_values = jnp.zeros((rows, LANES), jnp.float32)
        for head in range(heads):
            wanted = head // groups
            scores = dot(keys, qt_sc[head]) + bias
            probability = jnp.exp(scores - logs[head : head + 1])
            grad_values += dot(probability.astype(jnp.bfloat16), g_sc[head])
            grad_prob = dot(values, gt_sc[head])
            grad_scores = (probability * (grad_prob - deltas[head : head + 1])).astype(
                jnp.bfloat16
            )
            grad_keys += dot(grad_scores, q_sc[head])
            acc[head * HD : (head + 1) * HD] += dot(
                keys_turned[wanted * HD : (wanted + 1) * HD], grad_scores
            )
        gkv_ref[pl.ds(first, rows), :LANES] = grad_keys.astype(jnp.bfloat16)
        gkv_ref[pl.ds(first, rows), LANES:] = grad_values.astype(jnp.bfloat16)

    gq_ref[...] = (acc[...].T * HD ** (-0.5)).astype(jnp.bfloat16)


def norm_back(stream, scale, gain, grad_normed):
    inner = grad_normed * gain
    grad_gain = jnp.sum(grad_normed * stream * scale, axis=0)
    grad_stream = scale * inner - stream * scale * scale * scale * jnp.mean(
        stream * inner, axis=-1, keepdims=True
    )
    return (grad_stream, grad_gain)


def per_device(
    tokens,
    segments,
    routes,
    w_query,
    w_key,
    w_value,
    w_out,
    w_router,
    gain_attn,
    gain_ffn,
    w_gate,
    w_up,
    w_down,
    cotangent,
):
    head_count = lax.axis_size("head")
    cycle_count = lax.axis_size("blk")
    cycle_index = lax.axis_index("blk")
    local_tokens = tokens.shape[0]
    block_rows = local_tokens * head_count
    query_start = cycle_index * block_rows
    groups = H // KVH
    key_heads = KVH // head_count
    query_cols = H * HD // head_count
    key_cols = KVH * HD // head_count
    qkv_cols = query_cols + 2 * key_cols
    local_experts = E // head_count
    copies = cycle_count // local_experts
    copy_index = cycle_index % copies
    shard_rows = w_query.shape[1]
    slice_rows = w_gate.shape[2]
    hidden_units = w_gate.shape[3]
    score_scale = HD ** (-0.5)
    cosine_table, sine_table = rotary_tables(query_start, block_rows, HD)
    query_segs = lax.dynamic_slice_in_dim(segments, query_start, block_rows)
    block_last = segments.reshape(cycle_count, block_rows)[:, block_rows - 1]
    first_owner = jnp.sum(
        (block_last < query_segs[0]) & (jnp.arange(cycle_count) < cycle_index)
    ).astype(jnp.int32)

    hot = jnp.any(
        routes.T[None, :, :] == jnp.arange(E, dtype=jnp.int32)[:, None, None], axis=1
    )
    earlier = jnp.triu(jnp.ones((local_tokens, local_tokens), jnp.bfloat16), 1)
    slot = dot(hot.astype(jnp.bfloat16), earlier).astype(jnp.int32)
    picks = hot[:, None, :] & (
        slot[:, None, :] == jnp.arange(CAP, dtype=jnp.int32)[None, :, None]
    )
    picks_mat = picks.astype(jnp.bfloat16).reshape(E * CAP, local_tokens)

    def to_experts(rows):
        if copies > 1:
            mine = jnp.arange(copies)[None, :, None, None] == copy_index
            rows = jnp.where(mine, rows.reshape(E, 1, CAP, D), jnp.zeros((), rows.dtype))
            rows = rows.reshape(E * copies * CAP, D)
        return lax.all_to_all(rows, BOTH, split_axis=0, concat_axis=0, tiled=True)

    def from_experts(rows):
        rows = lax.all_to_all(rows, BOTH, split_axis=0, concat_axis=0, tiled=True)
        if copies > 1:
            rows = lax.dynamic_index_in_dim(
                rows.reshape(E, copies, CAP, D), copy_index, 1, keepdims=False
            ).reshape(E * CAP, D)
        return rows

    def by_head(values, cols):
        return values.reshape(LAYERS, shard_rows, head_count, cols)

    side = jnp.concatenate([w_router, gain_attn[..., None], gain_ffn[..., None]], axis=-1)
    side = jnp.pad(side, ((0, 0), (0, 0), (0, SIDE - side.shape[-1])))
    side = jnp.broadcast_to(side[:, :, None, :], (LAYERS, shard_rows, head_count, SIDE))
    sent = jnp.concatenate(
        [
            by_head(w_query, query_cols),
            by_head(w_key, key_cols),
            by_head(w_value, key_cols),
            side,
            jnp.broadcast_to(w_out[:, :, None, :], (LAYERS, shard_rows, head_count, D)),
        ],
        axis=-1,
    )
    sent = jnp.transpose(sent, (2, 0, 1, 3))
    sent = lax.all_to_all(sent, "head", split_axis=0, concat_axis=0, tiled=True)

    def gather_rows(part):
        mats = lax.all_gather(part, "blk", axis=0, tiled=False)
        return jnp.transpose(mats, (1, 0, 2, 3)).reshape(D, part.shape[-1])

    attn_all = []
    out_all = []
    for layer_index in range(LAYERS):
        if layer_index == 0:
            attn_all.append(gather_rows(sent[:, layer_index, :, : qkv_cols + SIDE]))
            out_all.append(gather_rows(sent[:, layer_index, :, qkv_cols + SIDE :]))
        else:
            mats = gather_rows(sent[:, layer_index])
            attn_all.append(mats[:, : qkv_cols + SIDE])
            out_all.append(mats[:, qkv_cols + SIDE :])
    tokens_block = lax.all_gather(tokens, "head", axis=0, tiled=True).astype(jnp.float32)

    def exchange_experts(layer_index):
        mats = jnp.stack([w_gate[layer_index], w_up[layer_index], w_down[layer_index]], axis=1)
        mats = jnp.repeat(mats, copies, axis=0)
        return lax.all_to_all(mats, "blk", split_axis=0, concat_axis=0, tiled=True)

    def expert_parts(mats):
        mats = jnp.transpose(mats, (1, 0, 2, 3)).reshape(3, D, hidden_units)
        return (mats[0], mats[1], mats[2])

    def exchange_grads(grads):
        grads = jnp.stack(grads).astype(jnp.bfloat16)
        grads = grads.reshape(3, cycle_count, slice_rows, hidden_units)
        grads = jnp.transpose(grads, (1, 0, 2, 3))
        return lax.all_to_all(grads, "blk", split_axis=0, concat_axis=0, tiled=True)

    def grad_parts(grads):
        grads = grads.reshape(local_experts, copies, 3, slice_rows, hidden_units)
        grads = jnp.sum(grads.astype(jnp.float32), axis=1)
        return (grads[:, 0], grads[:, 1], grads[:, 2])

    def sum_over_head(partial):
        parts = lax.all_to_all(
            partial.astype(jnp.bfloat16), "head", split_axis=0, concat_axis=0, tiled=True
        ).reshape(head_count, local_tokens, D)
        return jnp.sum(parts.astype(jnp.float32), axis=0)

    local_heads = H // head_count
    bounds = jnp.stack([first_owner, cycle_index + 1, query_start]).astype(jnp.int32)
    starts = jnp.sum(
        (segments[None, :] < query_segs[:, None]).astype(jnp.int32), axis=1, dtype=jnp.int32
    )
    in_smem = pl.BlockSpec(memory_space=pltpu.SMEM)
    in_vmem = pl.BlockSpec(memory_space=pltpu.VMEM)

    def widen(keys_all):
        parts = keys_all.reshape(-1, 2, key_cols)
        parts = jnp.pad(parts, ((0, 0), (0, 0), (0, LANES - key_cols)))
        return parts.reshape(-1, 2 * LANES)

    def narrow(key_grads):
        return key_grads.reshape(-1, 2, LANES)[:, :, :key_cols].reshape(-1, 2 * key_cols)

    def attend(queries, keys_wide):
        total_rows = keys_wide.shape[0]
        return pl.pallas_call(
            functools.partial(attend_kernel, local_heads, groups),
            out_shape=(
                jax.ShapeDtypeStruct((block_rows, query_cols), jnp.bfloat16),
                jax.ShapeDtypeStruct((SUBLANES, block_rows), jnp.float32),
            ),
            in_specs=[in_smem, in_vmem, in_vmem, in_vmem],
            out_specs=(in_vmem, in_vmem),
            scratch_shapes=[
                pltpu.VMEM((local_heads, LANES, block_rows), jnp.bfloat16),
                pltpu.VMEM((SUBLANES, block_rows), jnp.float32),
                pltpu.VMEM((SUBLANES, block_rows), jnp.float32),
                pltpu.VMEM((query_cols, block_rows), jnp.float32),
            ],
            cost_estimate=pl.CostEstimate(
                flops=2 * block_rows * total_rows * LANES * local_heads,
                bytes_accessed=2 * total_rows * 2 * LANES,
                transcendentals=block_rows * total_rows * local_heads,
            ),
            name="attend",
        )(bounds, queries, keys_wide, starts[None, :])

    def attend_back(queries, keys_wide, attended, log_total, grad_attended, beside):
        total_rows = keys_wide.shape[0]
        scratch = [pltpu.VMEM((local_heads, block_rows, LANES), jnp.bfloat16)]
        turned = [pltpu.VMEM((local_heads, LANES, block_rows), jnp.bfloat16)]
        grad_query, key_grads = pl.pallas_call(
            functools.partial(attend_back_kernel, local_heads, groups),
            out_shape=(
                jax.ShapeDtypeStruct((block_rows, query_cols), jnp.bfloat16),
                jax.ShapeDtypeStruct((total_rows, 2 * LANES), jnp.bfloat16),
            ),
            in_specs=[in_smem] + [in_vmem] * 6,
            out_specs=(in_vmem, in_vmem),
            scratch_shapes=(scratch + turned) * 2
            + [pltpu.VMEM((query_cols, block_rows), jnp.float32)],
            cost_estimate=pl.CostEstimate(
                flops=5 * block_rows * total_rows * LANES * local_heads,
                bytes_accessed=4 * total_rows * 2 * LANES,
                transcendentals=block_rows * total_rows * local_heads,
            ),
            name="attend_back",
        )(bounds, queries, keys_wide, starts[None, :], attended, log_total, grad_attended)
        grad_query, key_grads, beside = lax.optimization_barrier((grad_query, key_grads, beside))
        key_grads = lax.all_to_all(
            narrow(key_grads), "blk", split_axis=0, concat_axis=0, tiled=True
        )
        key_grads = jnp.sum(
            key_grads.reshape(cycle_count, block_rows, 2 * key_cols).astype(jnp.float32), axis=0
        ).astype(jnp.bfloat16)
        return (grad_query, key_grads, beside)

    stream = tokens.astype(jnp.float32)
    saved = []
    for layer_index in range(LAYERS):
        qkv_mat = attn_all[layer_index][:, :qkv_cols]
        side_all = attn_all[layer_index][:, qkv_cols:]
        router = side_all[:, :E]
        gain_first = side_all[:, E].astype(jnp.float32)
        gain_second = side_all[:, E + 1].astype(jnp.float32)
        out_mat = out_all[layer_index]
        scale_first = rms_scale(stream)
        if layer_index == 0:
            normed_block = (tokens_block * rms_scale(tokens_block) * gain_first).astype(
                jnp.bfloat16
            )
        else:
            normed_attn = (stream * scale_first * gain_first).astype(jnp.bfloat16)
            normed_block = lax.all_gather(normed_attn, "head", axis=0, tiled=True)
        qkv_pre = dot(normed_block, qkv_mat)
        query_pre = qkv_pre[:, :query_cols].reshape(block_rows, H // head_count, HD)
        key_pre = qkv_pre[:, query_cols : query_cols + key_cols].reshape(block_rows, key_heads, HD)
        queries = (
            rotate(query_pre, cosine_table, sine_table)
            .astype(jnp.bfloat16)
            .reshape(block_rows, query_cols)
        )
        key_rot = rotate(key_pre, cosine_table, sine_table).reshape(block_rows, key_cols)
        key_value = jnp.concatenate(
            [key_rot, qkv_pre[:, query_cols + key_cols :]], axis=1
        ).astype(jnp.bfloat16)
        keys_all = widen(lax.all_gather(key_value, "blk", axis=0, tiled=True))
        attended, log_total = attend(queries, keys_all)
        attended, expert_mats = lax.optimization_barrier(
            (attended, exchange_experts(layer_index))
        )
        gate_mat, up_mat, down_mat = expert_parts(expert_mats)
        attended_tok = lax.all_to_all(attended, "head", split_axis=0, concat_axis=1, tiled=True)
        middle = stream + dot(attended_tok, out_mat)
        scale_second = rms_scale(middle)
        normed_ffn = (middle * scale_second * gain_second).astype(jnp.bfloat16)
        logits = lax.dot_general(
            router, normed_ffn, (((0,), (1,)), ((), ())), preferred_element_type=jnp.float32
        )
        top = jnp.max(jnp.where(hot, logits, -jnp.inf), axis=0, keepdims=True)
        weight = jnp.where(hot, jnp.exp(jnp.where(hot, logits - top, 0.0)), 0.0)
        gate_prob = weight / jnp.sum(weight, axis=0, keepdims=True)
        arrived = to_experts(dot(picks_mat, normed_ffn).astype(jnp.bfloat16))
        gate_pre = dot(arrived, gate_mat)
        up_pre = dot(arrived, up_mat)
        hidden = (jax.nn.silu(gate_pre) * up_pre).astype(jnp.bfloat16)
        result = contract_cols(hidden, down_mat).astype(jnp.bfloat16)
        returned = from_experts(result)
        gate_rows = jnp.where(picks, gate_prob[:, None, :], 0.0).reshape(E * CAP, local_tokens)
        gate_high, gate_low = halves(gate_rows)
        saved.append(
            (
                stream,
                scale_first,
                normed_block,
                queries,
                keys_all,
                attended,
                log_total,
                middle,
                scale_second,
                normed_ffn,
                gate_prob,
                gate_rows,
                returned,
                arrived,
                gate_pre,
                up_pre,
                hidden,
                (qkv_mat, router, gain_first, gain_second, out_mat, gate_mat, up_mat, down_mat),
            )
        )
        stream = middle + contract_rows(gate_high, returned) + contract_rows(gate_low, returned)
    grad_stream = cotangent.astype(jnp.float32)
    layer_grads = [None] * LAYERS
    mats_grads = [None] * LAYERS
    out_grads = [None] * LAYERS
    earlier_sums = ()
    for layer_index in range(LAYERS - 1, -1, -1):
        (
            stream_in,
            scale_first,
            normed_block,
            queries,
            keys_all,
            attended,
            log_total,
            middle,
            scale_second,
            normed_ffn,
            gate_prob,
            gate_rows,
            returned,
            arrived,
            gate_pre,
            up_pre,
            hidden,
            (qkv_mat, router, gain_first, gain_second, out_mat, gate_mat, up_mat, down_mat),
        ) = saved[layer_index]
        grad_high, grad_low = halves(grad_stream)
        spread = dot(picks_mat, grad_high) + dot(picks_mat, grad_low)
        row_gate = jnp.sum(gate_rows, axis=1, keepdims=True)
        grad_result = to_experts((spread * row_gate).astype(jnp.bfloat16))
        if earlier_sums:
            grad_result, out_grads[layer_index + 1] = lax.optimization_barrier(
                (grad_result, earlier_sums[1])
            )
        row_choice = contract_cols(returned, grad_high) + contract_cols(returned, grad_low)
        grad_choice = jnp.sum(
            jnp.where(picks, row_choice.reshape(E, CAP, local_tokens), 0.0), axis=1
        )
        grad_hidden = dot(grad_result, down_mat)
        gate_sig = jax.nn.sigmoid(gate_pre)
        grad_gate_pre = (
            grad_hidden * up_pre * gate_sig * (1.0 + gate_pre * (1.0 - gate_sig))
        ).astype(jnp.bfloat16)
        grad_up_pre = (grad_hidden * gate_pre * gate_sig).astype(jnp.bfloat16)
        grad_arrived = (
            contract_cols(grad_gate_pre, gate_mat) + contract_cols(grad_up_pre, up_mat)
        ).astype(jnp.bfloat16)
        grad_rows = from_experts(grad_arrived)
        if earlier_sums:
            grad_rows, mats_grads[layer_index + 1] = lax.optimization_barrier(
                (grad_rows, earlier_sums[0])
            )
        expert_grads = exchange_grads(
            [
                contract_rows(arrived, grad_gate_pre),
                contract_rows(arrived, grad_up_pre),
                contract_rows(grad_result, hidden),
            ]
        )
        grad_normed = contract_rows(picks_mat, grad_rows)
        grad_logits = gate_prob * (
            grad_choice - jnp.sum(gate_prob * grad_choice, axis=0, keepdims=True)
        )
        grad_normed = grad_normed + lax.dot_general(
            grad_logits,
            router.astype(jnp.float32),
            (((0,), (1,)), ((), ())),
            precision=PRECISE,
        )
        grad_router = lax.dot_general(
            normed_ffn.astype(jnp.float32),
            grad_logits,
            (((0,), (1,)), ((), ())),
            precision=PRECISE,
        )
        grad_middle, grad_gain_second = norm_back(middle, scale_second, gain_second, grad_normed)
        grad_stream = grad_stream + grad_middle
        grad_branch = grad_stream.astype(jnp.bfloat16)
        grad_attended = contract_cols(grad_branch, out_mat).astype(jnp.bfloat16)
        grad_attended = lax.all_to_all(
            grad_attended, "head", split_axis=1, concat_axis=0, tiled=True
        )
        branch_block = lax.all_gather(grad_branch, "head", axis=0, tiled=True)
        grad_query, grad_kv, (expert_grads, branch_block) = attend_back(
            queries, keys_all, attended, log_total, grad_attended, (expert_grads, branch_block)
        )
        grad_out = contract_rows(attended, branch_block)
        grad_query_pre = (
            rotate(
                grad_query.reshape(block_rows, H // head_count, HD).astype(jnp.float32),
                cosine_table,
                -sine_table,
            )
            .astype(jnp.bfloat16)
            .reshape(block_rows, query_cols)
        )
        grad_key_pre = (
            rotate(
                grad_kv[:, :key_cols].reshape(block_rows, key_heads, HD).astype(jnp.float32),
                cosine_table,
                -sine_table,
            )
            .astype(jnp.bfloat16)
            .reshape(block_rows, key_cols)
        )
        grad_qkv = jnp.concatenate([grad_query_pre, grad_key_pre, grad_kv[:, key_cols:]], axis=1)
        grad_partial = contract_cols(grad_qkv, qkv_mat)
        grad_normed = sum_over_head(grad_partial)
        grad_gain_first = (
            jnp.sum(grad_partial * normed_block.astype(jnp.float32), axis=0) / gain_first
        )
        grad_first = norm_back(stream_in, scale_first, gain_first, grad_normed)[0]
        grad_stream = grad_stream + grad_first
        grad_side = jnp.concatenate(
            [grad_router, grad_gain_first[:, None], grad_gain_second[:, None]], axis=1
        )
        grad_side = jnp.pad(grad_side, ((0, 0), (0, SIDE - grad_side.shape[1])))
        grad_mats = jnp.concatenate(
            [contract_rows(normed_block, grad_qkv), grad_side], axis=1
        ).astype(jnp.bfloat16)
        grad_mats = jnp.transpose(
            grad_mats.reshape(head_count, cycle_count, shard_rows, qkv_cols + SIDE), (1, 0, 2, 3)
        ).reshape(cycle_count * head_count * shard_rows, qkv_cols + SIDE)
        grad_mats = lax.psum_scatter(grad_mats, "blk", scatter_dimension=0, tiled=True)
        grad_out = lax.psum_scatter(
            grad_out.astype(jnp.bfloat16), "blk", scatter_dimension=0, tiled=True
        )
        earlier_sums = (grad_mats, grad_out)
        layer_grads[layer_index] = grad_parts(expert_grads)
    mats_grads[0], out_grads[0] = earlier_sums
    mats_grads = jnp.stack(
        [sums.reshape(head_count, shard_rows, qkv_cols + SIDE) for sums in mats_grads], axis=1
    )
    mats_grads = lax.all_to_all(
        mats_grads, "head", split_axis=0, concat_axis=0, tiled=True
    ).astype(jnp.float32)

    def joined(start, stop):
        return jnp.transpose(mats_grads[..., start:stop], (1, 2, 0, 3)).reshape(
            LAYERS, shard_rows, -1
        )

    grad_side = jnp.sum(mats_grads[..., qkv_cols:], axis=0)
    gate_grads, up_grads, down_grads = [
        jnp.stack([layer_grads[layer_index][member] for layer_index in range(LAYERS)])
        for member in range(3)
    ]
    return (
        stream,
        grad_stream,
        joined(0, query_cols),
        joined(query_cols, query_cols + key_cols),
        joined(query_cols + key_cols, qkv_cols),
        jnp.stack(out_grads).astype(jnp.float32),
        grad_side[..., :E],
        grad_side[..., E],
        grad_side[..., E + 1],
        gate_grads,
        up_grads,
        down_grads,
    )


def solution(mesh):
    return jax.shard_map(
        per_device,
        mesh=mesh,
        in_specs=(
            P(("blk", "head"), None),
            P(),
            P(("blk", "head"), None),
            P(None, ("head", "blk"), None),
            P(None, ("head", "blk"), None),
            P(None, ("head", "blk"), None),
            P(None, ("head", "blk"), None),
            P(None, ("head", "blk"), None),
            P(None, ("head", "blk")),
            P(None, ("head", "blk")),
            P(None, "head", "blk", None),
            P(None, "head", "blk", None),
            P(None, "head", "blk", None),
            P(("blk", "head"), None),
        ),
        out_specs=(
            P(("blk", "head"), None),
            P(("blk", "head"), None),
            P(None, ("head", "blk"), None),
            P(None, ("head", "blk"), None),
            P(None, ("head", "blk"), None),
            P(None, ("head", "blk"), None),
            P(None, ("head", "blk"), None),
            P(None, ("head", "blk")),
            P(None, ("head", "blk")),
            P(None, "head", "blk", None),
            P(None, "head", "blk", None),
            P(None, "head", "blk", None),
        ),
        check_vma=False,
    )
```

```python
import functools

import jax
import jax.numpy as jnp
from jax import lax
from jax.experimental import pallas as pl
from jax.experimental.pallas import tpu as pltpu
from jax.sharding import PartitionSpec as P

D = 1024
H = 16
KVH = 8
HD = 64
E = 32
LAYERS = 2
CAP = 40
SIDE = 128
LANES = 128
SUBLANES = 8


EPSILON = 1e-06
MASKED = -1e30
ROPE_BASE = 10000.0
PRECISE = lax.Precision.HIGHEST
BOTH = ("head", "blk")


def rms_scale(values):
    return lax.rsqrt(jnp.mean(values * values, axis=-1, keepdims=True) + EPSILON)


def rotate(values, cosine_table, sine_table):
    half_dim = values.shape[-1] // 2
    first = values[..., :half_dim]
    second = values[..., half_dim:]
    return jnp.concatenate(
        [first * cosine_table - second * sine_table, second * cosine_table + first * sine_table],
        axis=-1,
    )


def rotary_tables(start, count, head_dim):
    half_dim = head_dim // 2
    frequency = jnp.power(ROPE_BASE, -(jnp.arange(half_dim, dtype=jnp.float32) * 2.0 / head_dim))
    places = start + jnp.arange(count, dtype=jnp.int32)
    angles = places.astype(jnp.float32)[:, None] * frequency[None, :]
    return (jnp.cos(angles)[:, None, :], jnp.sin(angles)[:, None, :])


def dot(left, right):
    return jnp.dot(left, right, preferred_element_type=jnp.float32)


def contract_rows(left, right, precision=None):
    return lax.dot_general(
        left,
        right,
        (((0,), (0,)), ((), ())),
        preferred_element_type=jnp.float32,
        precision=precision,
    )


def contract_cols(left, right, precision=None):
    return lax.dot_general(
        left,
        right,
        (((1,), (1,)), ((), ())),
        preferred_element_type=jnp.float32,
        precision=precision,
    )


def halves(values):
    high = lax.reduce_precision(values, 8, 7)
    return (high.astype(jnp.bfloat16), (values - high).astype(jnp.bfloat16))


def lane_half(shape):
    return lax.broadcasted_iota(jnp.int32, shape, 1) // HD


def head_lanes(values, head, groups):
    tile = values[:, head // 2 * LANES : (head // 2 + 1) * LANES]
    wanted = head // groups
    if head % 2 != wanted:
        tile = pltpu.roll(tile, HD, 1)
    return jnp.where(lane_half(tile.shape) == wanted, tile, 0.0)


def attend_kernel(
    heads, groups, bounds, q_ref, kv_ref, start_ref, o_ref, lse_ref, qt_sc, high, total, acc
):
    rows = q_ref.shape[0]
    scaled = q_ref[...].astype(jnp.float32) * HD ** (-0.5)
    for head in range(heads):
        qt_sc[head] = head_lanes(scaled, head, groups).T.astype(jnp.bfloat16)
    starts = start_ref[...]
    spots = bounds[2] + lax.broadcasted_iota(jnp.int32, (1, rows), 1)
    high[...] = jnp.full(high.shape, MASKED, jnp.float32)
    total[...] = jnp.ones(total.shape, jnp.float32)
    acc[...] = jnp.zeros(acc.shape, jnp.float32)

    @pl.loop(bounds[0], bounds[1])
    def _(owner):
        first = pl.multiple_of(owner * rows, rows)
        keys = kv_ref[pl.ds(first, rows), :LANES]
        values = kv_ref[pl.ds(first, rows), LANES:].astype(jnp.float32).T.astype(jnp.bfloat16)
        places = first + lax.broadcasted_iota(jnp.int32, (rows, rows), 0)
        bias = jnp.where((places >= starts) & (places <= spots), 0.0, MASKED)
        for head in range(heads):
            wanted = head // groups
            scores = dot(keys, qt_sc[head]) + bias
            old = high[head : head + 1]
            new = jnp.maximum(old, jnp.max(scores, axis=0, keepdims=True))
            exponent = jnp.exp(scores - new)
            factor = jnp.exp(old - new)
            total[head : head + 1] = total[head : head + 1] * factor + jnp.sum(
                exponent, axis=0, keepdims=True
            )
            acc[head * HD : (head + 1) * HD] = acc[head * HD : (head + 1) * HD] * factor + dot(
                values[wanted * HD : (wanted + 1) * HD], exponent.astype(jnp.bfloat16)
            )
            high[head : head + 1] = new

    lse_ref[...] = high[...] + jnp.log(total[...])
    for head in range(heads):
        acc[head * HD : (head + 1) * HD] = (
            acc[head * HD : (head + 1) * HD] / total[head : head + 1]
        )
    o_ref[...] = acc[...].T.astype(jnp.bfloat16)


def attend_back_kernel(
    heads,
    groups,
    bounds,
    q_ref,
    kv_ref,
    start_ref,
    o_ref,
    lse_ref,
    g_ref,
    gq_ref,
    gkv_ref,
    q_sc,
    qt_sc,
    g_sc,
    gt_sc,
    acc,
):
    rows = q_ref.shape[0]
    scaled = q_ref[...].astype(jnp.float32) * HD ** (-0.5)
    grads = g_ref[...].astype(jnp.float32)
    outs = o_ref[...].astype(jnp.float32)
    lanes = lax.broadcasted_iota(jnp.int32, (rows, LANES), 1)
    deltas = jnp.zeros((rows, LANES), jnp.float32)
    for head in range(heads):
        query = head_lanes(scaled, head, groups)
        q_sc[head] = query.astype(jnp.bfloat16)
        qt_sc[head] = query.T.astype(jnp.bfloat16)
        grad = head_lanes(grads, head, groups)
        g_sc[head] = grad.astype(jnp.bfloat16)
        gt_sc[head] = grad.T.astype(jnp.bfloat16)
        delta = jnp.sum(grad * head_lanes(outs, head, groups), axis=1, keepdims=True)
        deltas = jnp.where(lanes == head, delta, deltas)
    deltas = deltas.T
    logs = lse_ref[...]
    starts = start_ref[...]
    spots = bounds[2] + lax.broadcasted_iota(jnp.int32, (1, rows), 1)
    gkv_ref[...] = jnp.zeros(gkv_ref.shape, gkv_ref.dtype)
    acc[...] = jnp.zeros(acc.shape, jnp.float32)

    @pl.loop(bounds[0], bounds[1])
    def _(owner):
        first = pl.multiple_of(owner * rows, rows)
        keys = kv_ref[pl.ds(first, rows), :LANES]
        values = kv_ref[pl.ds(first, rows), LANES:]
        keys_turned = keys.astype(jnp.float32).T.astype(jnp.bfloat16)
        places = first + lax.broadcasted_iota(jnp.int32, (rows, rows), 0)
        bias = jnp.where((places >= starts) & (places <= spots), 0.0, MASKED)
        grad_keys = jnp.zeros((rows, LANES), jnp.float32)
        grad_values = jnp.zeros((rows, LANES), jnp.float32)
        for head in range(heads):
            wanted = head // groups
            scores = dot(keys, qt_sc[head]) + bias
            probability = jnp.exp(scores - logs[head : head + 1])
            grad_values += dot(probability.astype(jnp.bfloat16), g_sc[head])
            grad_prob = dot(values, gt_sc[head])
            grad_scores = (probability * (grad_prob - deltas[head : head + 1])).astype(
                jnp.bfloat16
            )
            grad_keys += dot(grad_scores, q_sc[head])
            acc[head * HD : (head + 1) * HD] += dot(
                keys_turned[wanted * HD : (wanted + 1) * HD], grad_scores
            )
        gkv_ref[pl.ds(first, rows), :LANES] = grad_keys.astype(jnp.bfloat16)
        gkv_ref[pl.ds(first, rows), LANES:] = grad_values.astype(jnp.bfloat16)

    gq_ref[...] = (acc[...].T * HD ** (-0.5)).astype(jnp.bfloat16)


def norm_back(stream, scale, gain, grad_normed):
    inner = grad_normed * gain
    grad_gain = jnp.sum(grad_normed * stream * scale, axis=0)
    grad_stream = scale * inner - stream * scale * scale * scale * jnp.mean(
        stream * inner, axis=-1, keepdims=True
    )
    return (grad_stream, grad_gain)


def per_device(
    tokens,
    segments,
    routes,
    w_query,
    w_key,
    w_value,
    w_out,
    w_router,
    gain_attn,
    gain_ffn,
    w_gate,
    w_up,
    w_down,
    cotangent,
):
    head_count = lax.axis_size("head")
    cycle_count = lax.axis_size("blk")
    cycle_index = lax.axis_index("blk")
    local_tokens = tokens.shape[0]
    block_rows = local_tokens * head_count
    query_start = cycle_index * block_rows
    groups = H // KVH
    key_heads = KVH // head_count
    query_cols = H * HD // head_count
    key_cols = KVH * HD // head_count
    qkv_cols = query_cols + 2 * key_cols
    local_experts = E // head_count
    copies = cycle_count // local_experts
    copy_index = cycle_index % copies
    shard_rows = w_query.shape[1]
    slice_rows = w_gate.shape[2]
    hidden_units = w_gate.shape[3]
    score_scale = HD ** (-0.5)
    cosine_table, sine_table = rotary_tables(query_start, block_rows, HD)
    query_segs = lax.dynamic_slice_in_dim(segments, query_start, block_rows)
    block_last = segments.reshape(cycle_count, block_rows)[:, block_rows - 1]
    first_owner = jnp.sum(
        (block_last < query_segs[0]) & (jnp.arange(cycle_count) < cycle_index)
    ).astype(jnp.int32)

    hot = jnp.any(
        routes.T[None, :, :] == jnp.arange(E, dtype=jnp.int32)[:, None, None], axis=1
    )
    earlier = jnp.triu(jnp.ones((local_tokens, local_tokens), jnp.bfloat16), 1)
    slot = dot(hot.astype(jnp.bfloat16), earlier).astype(jnp.int32)
    picks = hot[:, None, :] & (
        slot[:, None, :] == jnp.arange(CAP, dtype=jnp.int32)[None, :, None]
    )
    picks_mat = picks.astype(jnp.bfloat16).reshape(E * CAP, local_tokens)

    def to_experts(rows):
        if copies > 1:
            mine = jnp.arange(copies)[None, :, None, None] == copy_index
            rows = jnp.where(mine, rows.reshape(E, 1, CAP, D), jnp.zeros((), rows.dtype))
            rows = rows.reshape(E * copies * CAP, D)
        return lax.all_to_all(rows, BOTH, split_axis=0, concat_axis=0, tiled=True)

    def from_experts(rows):
        rows = lax.all_to_all(rows, BOTH, split_axis=0, concat_axis=0, tiled=True)
        if copies > 1:
            rows = lax.dynamic_index_in_dim(
                rows.reshape(E, copies, CAP, D), copy_index, 1, keepdims=False
            ).reshape(E * CAP, D)
        return rows

    def by_head(values):
        return values.reshape(shard_rows, head_count, -1)

    def for_all(values):
        return jnp.broadcast_to(values[:, None, :], (shard_rows, head_count, values.shape[-1]))

    def attn_parts(layer_index):
        side = jnp.concatenate(
            [
                w_router[layer_index],
                gain_attn[layer_index][:, None],
                gain_ffn[layer_index][:, None],
            ],
            axis=-1,
        )
        side = jnp.pad(side, ((0, 0), (0, SIDE - side.shape[-1])))
        return [
            by_head(w_query[layer_index]),
            by_head(w_key[layer_index]),
            by_head(w_value[layer_index]),
            for_all(side),
        ]

    def over_head(parts):
        parts = jnp.transpose(jnp.concatenate(parts, axis=-1), (1, 0, 2))
        return lax.all_to_all(parts, "head", split_axis=0, concat_axis=0, tiled=True)

    def gather_rows(part):
        mats = lax.all_gather(part, "blk", axis=0, tiled=False)
        return jnp.transpose(mats, (1, 0, 2, 3)).reshape(D, part.shape[-1])

    attn_cols = qkv_cols + SIDE
    attn_first = gather_rows(over_head(attn_parts(0)))
    tokens_block = lax.all_gather(tokens, "head", axis=0, tiled=True).astype(jnp.float32)

    def exchange_experts(layer_index):
        mats = jnp.stack([w_gate[layer_index], w_up[layer_index], w_down[layer_index]], axis=1)
        mats = jnp.repeat(mats, copies, axis=0)
        return lax.all_to_all(mats, "blk", split_axis=0, concat_axis=0, tiled=True)

    def expert_parts(mats):
        mats = jnp.transpose(mats, (1, 0, 2, 3)).reshape(3, D, hidden_units)
        return (mats[0], mats[1], mats[2])

    def exchange_grads(grads):
        grads = jnp.stack(grads).astype(jnp.bfloat16)
        grads = grads.reshape(-1, cycle_count, slice_rows, hidden_units)
        grads = jnp.transpose(grads, (1, 0, 2, 3))
        return lax.all_to_all(grads, "blk", split_axis=0, concat_axis=0, tiled=True)

    def grad_parts(grads):
        grads = grads.reshape(local_experts, copies, -1, slice_rows, hidden_units)
        grads = jnp.sum(grads.astype(jnp.float32), axis=1)
        return tuple(grads[:, member] for member in range(grads.shape[1]))

    def sum_over_head(partial):
        parts = lax.all_to_all(
            partial.astype(jnp.bfloat16), "head", split_axis=0, concat_axis=0, tiled=True
        ).reshape(head_count, local_tokens, D)
        return jnp.sum(parts.astype(jnp.float32), axis=0)

    local_heads = H // head_count
    bounds = jnp.stack([first_owner, cycle_index + 1, query_start]).astype(jnp.int32)
    starts = jnp.sum(
        (segments[None, :] < query_segs[:, None]).astype(jnp.int32), axis=1, dtype=jnp.int32
    )
    in_smem = pl.BlockSpec(memory_space=pltpu.SMEM)
    in_vmem = pl.BlockSpec(memory_space=pltpu.VMEM)

    def widen(keys_all):
        parts = keys_all.reshape(-1, 2, key_cols)
        parts = jnp.pad(parts, ((0, 0), (0, 0), (0, LANES - key_cols)))
        return parts.reshape(-1, 2 * LANES)

    def narrow(key_grads):
        return key_grads.reshape(-1, 2, LANES)[:, :, :key_cols].reshape(-1, 2 * key_cols)

    def attend(queries, keys_wide):
        total_rows = keys_wide.shape[0]
        return pl.pallas_call(
            functools.partial(attend_kernel, local_heads, groups),
            out_shape=(
                jax.ShapeDtypeStruct((block_rows, query_cols), jnp.bfloat16),
                jax.ShapeDtypeStruct((SUBLANES, block_rows), jnp.float32),
            ),
            in_specs=[in_smem, in_vmem, in_vmem, in_vmem],
            out_specs=(in_vmem, in_vmem),
            scratch_shapes=[
                pltpu.VMEM((local_heads, LANES, block_rows), jnp.bfloat16),
                pltpu.VMEM((SUBLANES, block_rows), jnp.float32),
                pltpu.VMEM((SUBLANES, block_rows), jnp.float32),
                pltpu.VMEM((query_cols, block_rows), jnp.float32),
            ],
            cost_estimate=pl.CostEstimate(
                flops=2 * block_rows * total_rows * LANES * local_heads,
                bytes_accessed=2 * total_rows * 2 * LANES,
                transcendentals=block_rows * total_rows * local_heads,
            ),
            name="attend",
        )(bounds, queries, keys_wide, starts[None, :])

    def attend_back(queries, keys_wide, attended, log_total, grad_attended, beside):
        total_rows = keys_wide.shape[0]
        scratch = [pltpu.VMEM((local_heads, block_rows, LANES), jnp.bfloat16)]
        turned = [pltpu.VMEM((local_heads, LANES, block_rows), jnp.bfloat16)]
        grad_query, key_grads = pl.pallas_call(
            functools.partial(attend_back_kernel, local_heads, groups),
            out_shape=(
                jax.ShapeDtypeStruct((block_rows, query_cols), jnp.bfloat16),
                jax.ShapeDtypeStruct((total_rows, 2 * LANES), jnp.bfloat16),
            ),
            in_specs=[in_smem] + [in_vmem] * 6,
            out_specs=(in_vmem, in_vmem),
            scratch_shapes=(scratch + turned) * 2
            + [pltpu.VMEM((query_cols, block_rows), jnp.float32)],
            cost_estimate=pl.CostEstimate(
                flops=5 * block_rows * total_rows * LANES * local_heads,
                bytes_accessed=4 * total_rows * 2 * LANES,
                transcendentals=block_rows * total_rows * local_heads,
            ),
            name="attend_back",
        )(bounds, queries, keys_wide, starts[None, :], attended, log_total, grad_attended)
        grad_query, key_grads, beside = lax.optimization_barrier((grad_query, key_grads, beside))
        key_grads = lax.all_to_all(
            narrow(key_grads), "blk", split_axis=0, concat_axis=0, tiled=True
        )
        key_grads = jnp.sum(
            key_grads.reshape(cycle_count, block_rows, 2 * key_cols).astype(jnp.float32), axis=0
        ).astype(jnp.bfloat16)
        return (grad_query, key_grads, beside)

    stream = tokens.astype(jnp.float32)
    saved = []
    for layer_index in range(LAYERS):
        if layer_index == 0:
            attn_mat, expert_mats = lax.optimization_barrier((attn_first, exchange_experts(0)))
        else:
            attn_mat = later_mats[layer_index][:, :attn_cols]
            out_mat = later_mats[layer_index][:, attn_cols:]
        qkv_mat = attn_mat[:, :qkv_cols]
        side_all = attn_mat[:, qkv_cols:]
        router = side_all[:, :E]
        gain_first = side_all[:, E].astype(jnp.float32)
        gain_second = side_all[:, E + 1].astype(jnp.float32)
        scale_first = rms_scale(stream)
        if layer_index == 0:
            normed_block = (tokens_block * rms_scale(tokens_block) * gain_first).astype(
                jnp.bfloat16
            )
        else:
            normed_attn = (stream * scale_first * gain_first).astype(jnp.bfloat16)
            normed_block = lax.all_gather(normed_attn, "head", axis=0, tiled=True)
        qkv_pre = dot(normed_block, qkv_mat)
        query_pre = qkv_pre[:, :query_cols].reshape(block_rows, H // head_count, HD)
        key_pre = qkv_pre[:, query_cols : query_cols + key_cols].reshape(block_rows, key_heads, HD)
        queries = (
            rotate(query_pre, cosine_table, sine_table)
            .astype(jnp.bfloat16)
            .reshape(block_rows, query_cols)
        )
        key_rot = rotate(key_pre, cosine_table, sine_table).reshape(block_rows, key_cols)
        key_value = jnp.concatenate(
            [key_rot, qkv_pre[:, query_cols + key_cols :]], axis=1
        ).astype(jnp.bfloat16)
        if layer_index > 0:
            key_value, expert_mats = lax.optimization_barrier(
                (key_value, exchange_experts(layer_index))
            )
        keys_all = lax.all_gather(key_value, "blk", axis=0, tiled=True)
        if layer_index == 0:
            rest = [for_all(w_out[0])]
            for later in range(1, LAYERS):
                rest += attn_parts(later) + [for_all(w_out[later])]
            keys_all, rest = lax.optimization_barrier((keys_all, over_head(rest)))
            out_mat = gather_rows(rest[..., :D])
            later_mats = [None]
            for later in range(1, LAYERS):
                begin = D + (later - 1) * (attn_cols + D)
                later_mats.append(gather_rows(rest[..., begin : begin + attn_cols + D]))
        keys_all = widen(keys_all)
        attended, log_total = attend(queries, keys_all)
        gate_mat, up_mat, down_mat = expert_parts(expert_mats)
        attended_tok = lax.all_to_all(attended, "head", split_axis=0, concat_axis=1, tiled=True)
        middle = stream + dot(attended_tok, out_mat)
        scale_second = rms_scale(middle)
        normed_ffn = (middle * scale_second * gain_second).astype(jnp.bfloat16)
        logits = lax.dot_general(
            router, normed_ffn, (((0,), (1,)), ((), ())), preferred_element_type=jnp.float32
        )
        top = jnp.max(jnp.where(hot, logits, -jnp.inf), axis=0, keepdims=True)
        weight = jnp.where(hot, jnp.exp(jnp.where(hot, logits - top, 0.0)), 0.0)
        gate_prob = weight / jnp.sum(weight, axis=0, keepdims=True)
        arrived = to_experts(dot(picks_mat, normed_ffn).astype(jnp.bfloat16))
        gate_pre = dot(arrived, gate_mat)
        up_pre = dot(arrived, up_mat)
        hidden = (jax.nn.silu(gate_pre) * up_pre).astype(jnp.bfloat16)
        result = contract_cols(hidden, down_mat).astype(jnp.bfloat16)
        returned = from_experts(result)
        gate_rows = jnp.where(picks, gate_prob[:, None, :], 0.0).reshape(E * CAP, local_tokens)
        gate_high, gate_low = halves(gate_rows)
        saved.append(
            (
                stream,
                scale_first,
                normed_block,
                queries,
                keys_all,
                attended,
                log_total,
                middle,
                scale_second,
                normed_ffn,
                gate_prob,
                gate_rows,
                returned,
                arrived,
                gate_pre,
                up_pre,
                hidden,
                (qkv_mat, router, gain_first, gain_second, out_mat, gate_mat, up_mat, down_mat),
            )
        )
        stream = middle + contract_rows(gate_high, returned) + contract_rows(gate_low, returned)
    grad_stream = cotangent.astype(jnp.float32)
    layer_grads = [None] * LAYERS
    mats_grads = [None] * LAYERS
    out_grads = [None] * LAYERS
    earlier_sums = ()
    for layer_index in range(LAYERS - 1, -1, -1):
        (
            stream_in,
            scale_first,
            normed_block,
            queries,
            keys_all,
            attended,
            log_total,
            middle,
            scale_second,
            normed_ffn,
            gate_prob,
            gate_rows,
            returned,
            arrived,
            gate_pre,
            up_pre,
            hidden,
            (qkv_mat, router, gain_first, gain_second, out_mat, gate_mat, up_mat, down_mat),
        ) = saved[layer_index]
        grad_high, grad_low = halves(grad_stream)
        spread = dot(picks_mat, grad_high) + dot(picks_mat, grad_low)
        row_gate = jnp.sum(gate_rows, axis=1, keepdims=True)
        grad_result = to_experts((spread * row_gate).astype(jnp.bfloat16))
        if earlier_sums:
            grad_result, out_grads[layer_index + 1] = lax.optimization_barrier(
                (grad_result, earlier_sums[1])
            )
        row_choice = contract_cols(returned, grad_high) + contract_cols(returned, grad_low)
        grad_choice = jnp.sum(
            jnp.where(picks, row_choice.reshape(E, CAP, local_tokens), 0.0), axis=1
        )
        grad_hidden = dot(grad_result, down_mat)
        gate_sig = jax.nn.sigmoid(gate_pre)
        grad_gate_pre = (
            grad_hidden * up_pre * gate_sig * (1.0 + gate_pre * (1.0 - gate_sig))
        ).astype(jnp.bfloat16)
        grad_up_pre = (grad_hidden * gate_pre * gate_sig).astype(jnp.bfloat16)
        grad_arrived = (
            contract_cols(grad_gate_pre, gate_mat) + contract_cols(grad_up_pre, up_mat)
        ).astype(jnp.bfloat16)
        grad_rows = from_experts(grad_arrived)
        if earlier_sums:
            grad_rows, mats_grads[layer_index + 1] = lax.optimization_barrier(
                (grad_rows, earlier_sums[0])
            )
        down_grads = exchange_grads([contract_rows(grad_result, hidden)])
        gate_up_grads = exchange_grads(
            [contract_rows(arrived, grad_gate_pre), contract_rows(arrived, grad_up_pre)]
        )
        grad_normed = contract_rows(picks_mat, grad_rows)
        grad_logits = gate_prob * (
            grad_choice - jnp.sum(gate_prob * grad_choice, axis=0, keepdims=True)
        )
        grad_normed = grad_normed + lax.dot_general(
            grad_logits,
            router.astype(jnp.float32),
            (((0,), (1,)), ((), ())),
            precision=PRECISE,
        )
        grad_router = lax.dot_general(
            normed_ffn.astype(jnp.float32),
            grad_logits,
            (((0,), (1,)), ((), ())),
            precision=PRECISE,
        )
        grad_middle, grad_gain_second = norm_back(middle, scale_second, gain_second, grad_normed)
        grad_stream = grad_stream + grad_middle
        grad_branch = grad_stream.astype(jnp.bfloat16)
        grad_attended = contract_cols(grad_branch, out_mat).astype(jnp.bfloat16)
        grad_attended = lax.all_to_all(
            grad_attended, "head", split_axis=1, concat_axis=0, tiled=True
        )
        branch_block = lax.all_gather(grad_branch, "head", axis=0, tiled=True)
        grad_query, grad_kv, (down_grads, branch_block) = attend_back(
            queries, keys_all, attended, log_total, grad_attended, (down_grads, branch_block)
        )
        grad_out = contract_rows(attended, branch_block)
        grad_query_pre = (
            rotate(
                grad_query.reshape(block_rows, H // head_count, HD).astype(jnp.float32),
                cosine_table,
                -sine_table,
            )
            .astype(jnp.bfloat16)
            .reshape(block_rows, query_cols)
        )
        grad_key_pre = (
            rotate(
                grad_kv[:, :key_cols].reshape(block_rows, key_heads, HD).astype(jnp.float32),
                cosine_table,
                -sine_table,
            )
            .astype(jnp.bfloat16)
            .reshape(block_rows, key_cols)
        )
        grad_qkv = jnp.concatenate([grad_query_pre, grad_key_pre, grad_kv[:, key_cols:]], axis=1)
        grad_partial = contract_cols(grad_qkv, qkv_mat)
        if layer_index > 0:
            grad_normed = lax.psum_scatter(
                grad_partial.astype(jnp.bfloat16), "head", scatter_dimension=0, tiled=True
            )
            grad_normed, gate_up_grads = lax.optimization_barrier((grad_normed, gate_up_grads))
            grad_normed = grad_normed.astype(jnp.float32)
        else:
            grad_normed = sum_over_head(grad_partial)
            grad_normed, gate_up_grads = lax.optimization_barrier((grad_normed, gate_up_grads))
        grad_gain_first = (
            jnp.sum(grad_partial * normed_block.astype(jnp.float32), axis=0) / gain_first
        )
        grad_first = norm_back(stream_in, scale_first, gain_first, grad_normed)[0]
        grad_stream = grad_stream + grad_first
        grad_side = jnp.concatenate(
            [grad_router, grad_gain_first[:, None], grad_gain_second[:, None]], axis=1
        )
        grad_side = jnp.pad(grad_side, ((0, 0), (0, SIDE - grad_side.shape[1])))
        grad_mats = jnp.concatenate(
            [contract_rows(normed_block, grad_qkv), grad_side], axis=1
        ).astype(jnp.bfloat16)
        grad_mats = jnp.transpose(
            grad_mats.reshape(head_count, cycle_count, shard_rows, qkv_cols + SIDE), (1, 0, 2, 3)
        ).reshape(cycle_count * head_count * shard_rows, qkv_cols + SIDE)
        grad_mats = lax.psum_scatter(grad_mats, "blk", scatter_dimension=0, tiled=True)
        grad_out = lax.psum_scatter(
            grad_out.astype(jnp.bfloat16), "blk", scatter_dimension=0, tiled=True
        )
        earlier_sums = (grad_mats, grad_out)
        layer_grads[layer_index] = grad_parts(gate_up_grads) + grad_parts(down_grads)
    mats_grads[0], out_grads[0] = earlier_sums
    mats_grads = jnp.stack(
        [sums.reshape(head_count, shard_rows, qkv_cols + SIDE) for sums in mats_grads], axis=1
    )
    mats_grads = lax.all_to_all(
        mats_grads, "head", split_axis=0, concat_axis=0, tiled=True
    ).astype(jnp.float32)

    def joined(start, stop):
        return jnp.transpose(mats_grads[..., start:stop], (1, 2, 0, 3)).reshape(
            LAYERS, shard_rows, -1
        )

    grad_side = jnp.sum(mats_grads[..., qkv_cols:], axis=0)
    gate_grads, up_grads, down_grads = [
        jnp.stack([layer_grads[layer_index][member] for layer_index in range(LAYERS)])
        for member in range(3)
    ]
    return (
        stream,
        grad_stream,
        joined(0, query_cols),
        joined(query_cols, query_cols + key_cols),
        joined(query_cols + key_cols, qkv_cols),
        jnp.stack(out_grads).astype(jnp.float32),
        grad_side[..., :E],
        grad_side[..., E],
        grad_side[..., E + 1],
        gate_grads,
        up_grads,
        down_grads,
    )


def solution(mesh):
    return jax.shard_map(
        per_device,
        mesh=mesh,
        in_specs=(
            P(("blk", "head"), None),
            P(),
            P(("blk", "head"), None),
            P(None, ("head", "blk"), None),
            P(None, ("head", "blk"), None),
            P(None, ("head", "blk"), None),
            P(None, ("head", "blk"), None),
            P(None, ("head", "blk"), None),
            P(None, ("head", "blk")),
            P(None, ("head", "blk")),
            P(None, "head", "blk", None),
            P(None, "head", "blk", None),
            P(None, "head", "blk", None),
            P(("blk", "head"), None),
        ),
        out_specs=(
            P(("blk", "head"), None),
            P(("blk", "head"), None),
            P(None, ("head", "blk"), None),
            P(None, ("head", "blk"), None),
            P(None, ("head", "blk"), None),
            P(None, ("head", "blk"), None),
            P(None, ("head", "blk"), None),
            P(None, ("head", "blk")),
            P(None, ("head", "blk")),
            P(None, "head", "blk", None),
            P(None, "head", "blk", None),
            P(None, "head", "blk", None),
        ),
        check_vma=False,
    )
```

```python
import functools

import jax
import jax.numpy as jnp
from jax import lax
from jax.experimental import pallas as pl
from jax.experimental.pallas import tpu as pltpu
from jax.sharding import PartitionSpec as P

D = 1024
H = 16
KVH = 8
HD = 64
E = 32
LAYERS = 2
CAP = 40
SIDE = 128
LANES = 128
SUBLANES = 8


EPSILON = 1e-06
MASKED = -1e30
ROPE_BASE = 10000.0
PRECISE = lax.Precision.HIGHEST
BOTH = ("head", "blk")


def rms_scale(values):
    return lax.rsqrt(jnp.mean(values * values, axis=-1, keepdims=True) + EPSILON)


def rotary_tables(start, count):
    half_dim = HD // 2
    frequency = jnp.power(ROPE_BASE, -(jnp.arange(half_dim, dtype=jnp.float32) * 2.0 / HD))
    places = start + jnp.arange(count, dtype=jnp.int32)
    angles = places.astype(jnp.float32)[:, None] * frequency[None, :]
    cosine, sine = jnp.cos(angles), jnp.sin(angles)
    zero = jnp.zeros_like(sine)
    times = LANES // HD
    return jnp.stack(
        [
            jnp.concatenate([cosine, cosine] * times, axis=1),
            jnp.concatenate([zero, sine] * times, axis=1),
            jnp.concatenate([-sine, zero] * times, axis=1),
        ]
    )


def dot(left, right):
    return jnp.dot(left, right, preferred_element_type=jnp.float32)


def contract_rows(left, right, precision=None):
    return lax.dot_general(
        left,
        right,
        (((0,), (0,)), ((), ())),
        preferred_element_type=jnp.float32,
        precision=precision,
    )


def contract_cols(left, right, precision=None):
    return lax.dot_general(
        left,
        right,
        (((1,), (1,)), ((), ())),
        preferred_element_type=jnp.float32,
        precision=precision,
    )


def halves(values):
    high = lax.reduce_precision(values, 8, 7)
    return (high.astype(jnp.bfloat16), (values - high).astype(jnp.bfloat16))


def rotate_tile(tile, tables, sign, lanes_turned):
    turned = tile * tables[0] + sign * (
        pltpu.roll(tile, HD // 2, 1) * tables[1] + pltpu.roll(tile, LANES - HD // 2, 1) * tables[2]
    )
    if lanes_turned < LANES:
        lanes = lax.broadcasted_iota(jnp.int32, tile.shape, 1)
        turned = jnp.where(lanes < lanes_turned, turned, tile)
    return turned


def project_kernel(turned_cols, normed_ref, mat_ref, tables_ref, q_ref, kv_ref):
    query_cols = q_ref.shape[1]
    pre = dot(normed_ref[...], mat_ref[:, : query_cols + kv_ref.shape[1]])
    for begin in range(0, pre.shape[1], LANES):
        tile = pre[:, begin : begin + LANES]
        if begin < turned_cols:
            tile = rotate_tile(tile, tables_ref, 1.0, turned_cols - begin)
        tile = tile.astype(jnp.bfloat16)
        if begin < query_cols:
            q_ref[:, begin : begin + LANES] = tile
        else:
            kv_ref[:, begin - query_cols : begin - query_cols + LANES] = tile


def project_back_kernel(
    turned_cols,
    gq_ref,
    gkv_ref,
    normed_ref,
    mat_ref,
    tables_ref,
    gain_ref,
    side_ref,
    partial_ref,
    mats_ref,
    grad_sc,
):
    rows, query_cols = gq_ref.shape
    count, heads, shard_rows = mats_ref.shape[:3]
    sums = gkv_ref[:rows].astype(jnp.float32)
    for source in range(1, gkv_ref.shape[0] // rows):
        sums += gkv_ref[source * rows : (source + 1) * rows].astype(jnp.float32)
    sums = sums.astype(jnp.bfloat16).astype(jnp.float32)
    cols = query_cols + sums.shape[1]
    for begin in range(0, cols, LANES):
        if begin < query_cols:
            tile = gq_ref[:, begin : begin + LANES].astype(jnp.float32)
        else:
            tile = sums[:, begin - query_cols : begin - query_cols + LANES]
        if begin < turned_cols:
            tile = rotate_tile(tile, tables_ref, -1.0, turned_cols - begin)
        grad_sc[:, begin : begin + LANES] = tile.astype(jnp.bfloat16)
    grads = grad_sc[...]
    partial = contract_cols(grads, mat_ref[:, :cols])
    partial_ref[...] = partial.astype(jnp.bfloat16)
    gain = jnp.sum(partial * normed_ref[...].astype(jnp.float32), axis=0, keepdims=True)
    gain = gain / gain_ref[...]
    gain = jnp.broadcast_to(gain, (LANES, gain.shape[1])).T
    lanes = lax.broadcasted_iota(jnp.int32, gain.shape, 1)
    side = jnp.where(lanes == E, gain, side_ref[...]).astype(jnp.bfloat16)
    mats = contract_rows(normed_ref[...], grads).astype(jnp.bfloat16)
    for head in range(heads):
        for place in range(count):
            first = (head * count + place) * shard_rows
            mats_ref[place, head, :, :cols] = mats[first : first + shard_rows]
            mats_ref[place, head, :, cols:] = side[first : first + shard_rows]


def lane_half(shape):
    return lax.broadcasted_iota(jnp.int32, shape, 1) // HD


def head_lanes(values, head, groups):
    tile = values[:, head // 2 * LANES : (head // 2 + 1) * LANES]
    wanted = head // groups
    if head % 2 != wanted:
        tile = pltpu.roll(tile, HD, 1)
    return jnp.where(lane_half(tile.shape) == wanted, tile, 0.0)


def attend_kernel(
    heads, groups, bounds, q_ref, kv_ref, start_ref, o_ref, lse_ref, qt_sc, high, total, acc
):
    rows = q_ref.shape[0]
    scaled = q_ref[...].astype(jnp.float32) * HD ** (-0.5)
    for head in range(heads):
        qt_sc[head] = head_lanes(scaled, head, groups).T.astype(jnp.bfloat16)
    starts = start_ref[...]
    spots = bounds[2] + lax.broadcasted_iota(jnp.int32, (1, rows), 1)
    high[...] = jnp.full(high.shape, MASKED, jnp.float32)
    total[...] = jnp.ones(total.shape, jnp.float32)
    acc[...] = jnp.zeros(acc.shape, jnp.float32)

    @pl.loop(bounds[0], bounds[1])
    def _(owner):
        first = pl.multiple_of(owner * rows, rows)
        keys = kv_ref[pl.ds(first, rows), :LANES]
        values = kv_ref[pl.ds(first, rows), LANES:].astype(jnp.float32).T.astype(jnp.bfloat16)
        places = first + lax.broadcasted_iota(jnp.int32, (rows, rows), 0)
        bias = jnp.where((places >= starts) & (places <= spots), 0.0, MASKED)
        for head in range(heads):
            wanted = head // groups
            scores = dot(keys, qt_sc[head]) + bias
            old = high[head : head + 1]
            new = jnp.maximum(old, jnp.max(scores, axis=0, keepdims=True))
            exponent = jnp.exp(scores - new)
            factor = jnp.exp(old - new)
            total[head : head + 1] = total[head : head + 1] * factor + jnp.sum(
                exponent, axis=0, keepdims=True
            )
            acc[head * HD : (head + 1) * HD] = acc[head * HD : (head + 1) * HD] * factor + dot(
                values[wanted * HD : (wanted + 1) * HD], exponent.astype(jnp.bfloat16)
            )
            high[head : head + 1] = new

    lse_ref[...] = high[...] + jnp.log(total[...])
    for head in range(heads):
        acc[head * HD : (head + 1) * HD] = (
            acc[head * HD : (head + 1) * HD] / total[head : head + 1]
        )
    o_ref[...] = acc[...].T.astype(jnp.bfloat16)


def attend_back_kernel(
    heads,
    groups,
    bounds,
    q_ref,
    kv_ref,
    start_ref,
    o_ref,
    lse_ref,
    g_ref,
    gq_ref,
    gkv_ref,
    q_sc,
    qt_sc,
    g_sc,
    gt_sc,
    acc,
):
    rows = q_ref.shape[0]
    scaled = q_ref[...].astype(jnp.float32) * HD ** (-0.5)
    grads = g_ref[...].astype(jnp.float32)
    outs = o_ref[...].astype(jnp.float32)
    lanes = lax.broadcasted_iota(jnp.int32, (rows, LANES), 1)
    deltas = jnp.zeros((rows, LANES), jnp.float32)
    for head in range(heads):
        query = head_lanes(scaled, head, groups)
        q_sc[head] = query.astype(jnp.bfloat16)
        qt_sc[head] = query.T.astype(jnp.bfloat16)
        grad = head_lanes(grads, head, groups)
        g_sc[head] = grad.astype(jnp.bfloat16)
        gt_sc[head] = grad.T.astype(jnp.bfloat16)
        delta = jnp.sum(grad * head_lanes(outs, head, groups), axis=1, keepdims=True)
        deltas = jnp.where(lanes == head, delta, deltas)
    deltas = deltas.T
    logs = lse_ref[...]
    starts = start_ref[...]
    spots = bounds[2] + lax.broadcasted_iota(jnp.int32, (1, rows), 1)
    gkv_ref[...] = jnp.zeros(gkv_ref.shape, gkv_ref.dtype)
    acc[...] = jnp.zeros(acc.shape, jnp.float32)

    @pl.loop(bounds[0], bounds[1])
    def _(owner):
        first = pl.multiple_of(owner * rows, rows)
        keys = kv_ref[pl.ds(first, rows), :LANES]
        values = kv_ref[pl.ds(first, rows), LANES:]
        keys_turned = keys.astype(jnp.float32).T.astype(jnp.bfloat16)
        places = first + lax.broadcasted_iota(jnp.int32, (rows, rows), 0)
        bias = jnp.where((places >= starts) & (places <= spots), 0.0, MASKED)
        grad_keys = jnp.zeros((rows, LANES), jnp.float32)
        grad_values = jnp.zeros((rows, LANES), jnp.float32)
        for head in range(heads):
            wanted = head // groups
            scores = dot(keys, qt_sc[head]) + bias
            probability = jnp.exp(scores - logs[head : head + 1])
            grad_values += dot(probability.astype(jnp.bfloat16), g_sc[head])
            grad_prob = dot(values, gt_sc[head])
            grad_scores = (probability * (grad_prob - deltas[head : head + 1])).astype(
                jnp.bfloat16
            )
            grad_keys += dot(grad_scores, q_sc[head])
            acc[head * HD : (head + 1) * HD] += dot(
                keys_turned[wanted * HD : (wanted + 1) * HD], grad_scores
            )
        gkv_ref[pl.ds(first, rows), :LANES] = grad_keys.astype(jnp.bfloat16)
        gkv_ref[pl.ds(first, rows), LANES:] = grad_values.astype(jnp.bfloat16)

    gq_ref[...] = (acc[...].T * HD ** (-0.5)).astype(jnp.bfloat16)


def norm_back(stream, scale, gain, grad_normed):
    inner = grad_normed * gain
    grad_gain = jnp.sum(grad_normed * stream * scale, axis=0)
    grad_stream = scale * inner - stream * scale * scale * scale * jnp.mean(
        stream * inner, axis=-1, keepdims=True
    )
    return (grad_stream, grad_gain)


def per_device(
    tokens,
    segments,
    routes,
    w_query,
    w_key,
    w_value,
    w_out,
    w_router,
    gain_attn,
    gain_ffn,
    w_gate,
    w_up,
    w_down,
    cotangent,
):
    head_count = lax.axis_size("head")
    cycle_count = lax.axis_size("blk")
    cycle_index = lax.axis_index("blk")
    local_tokens = tokens.shape[0]
    block_rows = local_tokens * head_count
    query_start = cycle_index * block_rows
    groups = H // KVH
    key_heads = KVH // head_count
    query_cols = H * HD // head_count
    key_cols = KVH * HD // head_count
    qkv_cols = query_cols + 2 * key_cols
    local_experts = E // head_count
    copies = cycle_count // local_experts
    copy_index = cycle_index % copies
    shard_rows = w_query.shape[1]
    slice_rows = w_gate.shape[2]
    hidden_units = w_gate.shape[3]
    score_scale = HD ** (-0.5)
    tables = rotary_tables(query_start, block_rows)
    query_segs = lax.dynamic_slice_in_dim(segments, query_start, block_rows)
    block_last = segments.reshape(cycle_count, block_rows)[:, block_rows - 1]
    first_owner = jnp.sum(
        (block_last < query_segs[0]) & (jnp.arange(cycle_count) < cycle_index)
    ).astype(jnp.int32)

    hot = jnp.any(
        routes.T[None, :, :] == jnp.arange(E, dtype=jnp.int32)[:, None, None], axis=1
    )
    earlier = jnp.triu(jnp.ones((local_tokens, local_tokens), jnp.bfloat16), 1)
    slot = dot(hot.astype(jnp.bfloat16), earlier).astype(jnp.int32)
    picks = hot[:, None, :] & (
        slot[:, None, :] == jnp.arange(CAP, dtype=jnp.int32)[None, :, None]
    )
    picks_mat = picks.astype(jnp.bfloat16).reshape(E * CAP, local_tokens)

    def to_experts(rows):
        if copies > 1:
            mine = jnp.arange(copies)[None, :, None, None] == copy_index
            rows = jnp.where(mine, rows.reshape(E, 1, CAP, D), jnp.zeros((), rows.dtype))
            rows = rows.reshape(E * copies * CAP, D)
        return lax.all_to_all(rows, BOTH, split_axis=0, concat_axis=0, tiled=True)

    def from_experts(rows):
        rows = lax.all_to_all(rows, BOTH, split_axis=0, concat_axis=0, tiled=True)
        if copies > 1:
            rows = lax.dynamic_index_in_dim(
                rows.reshape(E, copies, CAP, D), copy_index, 1, keepdims=False
            ).reshape(E * CAP, D)
        return rows

    def by_head(values):
        return values.reshape(shard_rows, head_count, -1)

    def for_all(values):
        return jnp.broadcast_to(values[:, None, :], (shard_rows, head_count, values.shape[-1]))

    def attn_parts(layer_index):
        side = jnp.concatenate(
            [
                w_router[layer_index],
                gain_attn[layer_index][:, None],
                gain_ffn[layer_index][:, None],
            ],
            axis=-1,
        )
        side = jnp.pad(side, ((0, 0), (0, SIDE - side.shape[-1])))
        return [
            by_head(w_query[layer_index]),
            by_head(w_key[layer_index]),
            by_head(w_value[layer_index]),
            for_all(side),
        ]

    def over_head(parts):
        parts = jnp.transpose(jnp.concatenate(parts, axis=-1), (1, 0, 2))
        return lax.all_to_all(parts, "head", split_axis=0, concat_axis=0, tiled=True)

    def gather_rows(part):
        mats = lax.all_gather(part, "blk", axis=0, tiled=False)
        return jnp.transpose(mats, (1, 0, 2, 3)).reshape(D, part.shape[-1])

    attn_cols = qkv_cols + SIDE
    attn_first = gather_rows(over_head(attn_parts(0)))
    tokens_block = lax.all_gather(tokens, "head", axis=0, tiled=True).astype(jnp.float32)

    def exchange_experts(layer_index):
        mats = jnp.stack([w_gate[layer_index], w_up[layer_index], w_down[layer_index]], axis=1)
        mats = jnp.repeat(mats, copies, axis=0)
        return lax.all_to_all(mats, "blk", split_axis=0, concat_axis=0, tiled=True)

    def expert_parts(mats):
        mats = jnp.transpose(mats, (1, 0, 2, 3)).reshape(3, D, hidden_units)
        return (mats[0], mats[1], mats[2])

    def exchange_grads(grads):
        grads = jnp.stack(grads).astype(jnp.bfloat16)
        grads = grads.reshape(-1, cycle_count, slice_rows, hidden_units)
        grads = jnp.transpose(grads, (1, 0, 2, 3))
        return lax.all_to_all(grads, "blk", split_axis=0, concat_axis=0, tiled=True)

    def grad_parts(grads):
        grads = grads.reshape(local_experts, copies, -1, slice_rows, hidden_units)
        grads = jnp.sum(grads.astype(jnp.float32), axis=1)
        return tuple(grads[:, member] for member in range(grads.shape[1]))

    def sum_over_head(partial):
        parts = lax.all_to_all(
            partial.astype(jnp.bfloat16), "head", split_axis=0, concat_axis=0, tiled=True
        ).reshape(head_count, local_tokens, D)
        return jnp.sum(parts.astype(jnp.float32), axis=0)

    local_heads = H // head_count
    bounds = jnp.stack([first_owner, cycle_index + 1, query_start]).astype(jnp.int32)
    starts = jnp.sum(
        (segments[None, :] < query_segs[:, None]).astype(jnp.int32), axis=1, dtype=jnp.int32
    )
    in_smem = pl.BlockSpec(memory_space=pltpu.SMEM)
    in_vmem = pl.BlockSpec(memory_space=pltpu.VMEM)

    def widen(keys_all):
        parts = keys_all.reshape(-1, 2, key_cols)
        parts = jnp.pad(parts, ((0, 0), (0, 0), (0, LANES - key_cols)))
        return parts.reshape(-1, 2 * LANES)

    def narrow(key_grads):
        return key_grads.reshape(-1, 2, LANES)[:, :, :key_cols].reshape(-1, 2 * key_cols)

    def attend(queries, keys_wide):
        total_rows = keys_wide.shape[0]
        return pl.pallas_call(
            functools.partial(attend_kernel, local_heads, groups),
            out_shape=(
                jax.ShapeDtypeStruct((block_rows, query_cols), jnp.bfloat16),
                jax.ShapeDtypeStruct((SUBLANES, block_rows), jnp.float32),
            ),
            in_specs=[in_smem, in_vmem, in_vmem, in_vmem],
            out_specs=(in_vmem, in_vmem),
            scratch_shapes=[
                pltpu.VMEM((local_heads, LANES, block_rows), jnp.bfloat16),
                pltpu.VMEM((SUBLANES, block_rows), jnp.float32),
                pltpu.VMEM((SUBLANES, block_rows), jnp.float32),
                pltpu.VMEM((query_cols, block_rows), jnp.float32),
            ],
            cost_estimate=pl.CostEstimate(
                flops=2 * block_rows * total_rows * LANES * local_heads,
                bytes_accessed=2 * total_rows * 2 * LANES,
                transcendentals=block_rows * total_rows * local_heads,
            ),
            name="attend",
        )(bounds, queries, keys_wide, starts[None, :])

    def project(normed_block, attn_mat):
        return pl.pallas_call(
            functools.partial(project_kernel, query_cols + key_cols),
            out_shape=(
                jax.ShapeDtypeStruct((block_rows, query_cols), jnp.bfloat16),
                jax.ShapeDtypeStruct((block_rows, 2 * key_cols), jnp.bfloat16),
            ),
            in_specs=[in_vmem] * 3,
            out_specs=(in_vmem, in_vmem),
            cost_estimate=pl.CostEstimate(
                flops=2 * block_rows * D * qkv_cols,
                bytes_accessed=2 * (block_rows + attn_cols) * D,
                transcendentals=0,
            ),
            name="project",
        )(normed_block, attn_mat, tables)

    def project_back(grad_query, grad_kv, normed_block, attn_mat, gain, grad_side):
        return pl.pallas_call(
            functools.partial(project_back_kernel, query_cols + key_cols),
            out_shape=(
                jax.ShapeDtypeStruct((block_rows, D), jnp.bfloat16),
                jax.ShapeDtypeStruct(
                    (cycle_count, head_count, shard_rows, attn_cols), jnp.bfloat16
                ),
            ),
            in_specs=[in_vmem] * 7,
            out_specs=(in_vmem, in_vmem),
            scratch_shapes=[pltpu.VMEM((block_rows, qkv_cols), jnp.bfloat16)],
            cost_estimate=pl.CostEstimate(
                flops=4 * block_rows * D * qkv_cols,
                bytes_accessed=2 * (block_rows + attn_cols) * D,
                transcendentals=0,
            ),
            name="project_back",
        )(grad_query, grad_kv, normed_block, attn_mat, tables, gain[None, :], grad_side)

    def attend_back(queries, keys_wide, attended, log_total, grad_attended, beside):
        total_rows = keys_wide.shape[0]
        scratch = [pltpu.VMEM((local_heads, block_rows, LANES), jnp.bfloat16)]
        turned = [pltpu.VMEM((local_heads, LANES, block_rows), jnp.bfloat16)]
        grad_query, key_grads = pl.pallas_call(
            functools.partial(attend_back_kernel, local_heads, groups),
            out_shape=(
                jax.ShapeDtypeStruct((block_rows, query_cols), jnp.bfloat16),
                jax.ShapeDtypeStruct((total_rows, 2 * LANES), jnp.bfloat16),
            ),
            in_specs=[in_smem] + [in_vmem] * 6,
            out_specs=(in_vmem, in_vmem),
            scratch_shapes=(scratch + turned) * 2
            + [pltpu.VMEM((query_cols, block_rows), jnp.float32)],
            cost_estimate=pl.CostEstimate(
                flops=5 * block_rows * total_rows * LANES * local_heads,
                bytes_accessed=4 * total_rows * 2 * LANES,
                transcendentals=block_rows * total_rows * local_heads,
            ),
            name="attend_back",
        )(bounds, queries, keys_wide, starts[None, :], attended, log_total, grad_attended)
        grad_query, key_grads, beside = lax.optimization_barrier((grad_query, key_grads, beside))
        key_grads = lax.all_to_all(
            narrow(key_grads), "blk", split_axis=0, concat_axis=0, tiled=True
        )
        return (grad_query, key_grads, beside)

    stream = tokens.astype(jnp.float32)
    saved = []
    for layer_index in range(LAYERS):
        if layer_index == 0:
            attn_mat, expert_mats = lax.optimization_barrier((attn_first, exchange_experts(0)))
        else:
            attn_mat = later_mats[layer_index][:, :attn_cols]
            out_mat = later_mats[layer_index][:, attn_cols:]
        side_all = attn_mat[:, qkv_cols:]
        router = side_all[:, :E]
        gain_first = side_all[:, E].astype(jnp.float32)
        gain_second = side_all[:, E + 1].astype(jnp.float32)
        scale_first = rms_scale(stream)
        if layer_index == 0:
            normed_block = (tokens_block * rms_scale(tokens_block) * gain_first).astype(
                jnp.bfloat16
            )
        else:
            normed_attn = (stream * scale_first * gain_first).astype(jnp.bfloat16)
            normed_block = lax.all_gather(normed_attn, "head", axis=0, tiled=True)
        queries, key_value = project(normed_block, attn_mat)
        if layer_index > 0:
            key_value, expert_mats = lax.optimization_barrier(
                (key_value, exchange_experts(layer_index))
            )
        keys_all = lax.all_gather(key_value, "blk", axis=0, tiled=True)
        if layer_index == 0:
            rest = [for_all(w_out[0])]
            for later in range(1, LAYERS):
                rest += attn_parts(later) + [for_all(w_out[later])]
            keys_all, rest = lax.optimization_barrier((keys_all, over_head(rest)))
            out_mat = gather_rows(rest[..., :D])
            later_mats = [None]
            for later in range(1, LAYERS):
                begin = D + (later - 1) * (attn_cols + D)
                later_mats.append(gather_rows(rest[..., begin : begin + attn_cols + D]))
        keys_all = widen(keys_all)
        attended, log_total = attend(queries, keys_all)
        gate_mat, up_mat, down_mat = expert_parts(expert_mats)
        attended_tok = lax.all_to_all(attended, "head", split_axis=0, concat_axis=1, tiled=True)
        middle = stream + dot(attended_tok, out_mat)
        scale_second = rms_scale(middle)
        normed_ffn = (middle * scale_second * gain_second).astype(jnp.bfloat16)
        logits = lax.dot_general(
            router, normed_ffn, (((0,), (1,)), ((), ())), preferred_element_type=jnp.float32
        )
        top = jnp.max(jnp.where(hot, logits, -jnp.inf), axis=0, keepdims=True)
        weight = jnp.where(hot, jnp.exp(jnp.where(hot, logits - top, 0.0)), 0.0)
        gate_prob = weight / jnp.sum(weight, axis=0, keepdims=True)
        arrived = to_experts(dot(picks_mat, normed_ffn).astype(jnp.bfloat16))
        gate_pre = dot(arrived, gate_mat)
        up_pre = dot(arrived, up_mat)
        hidden = (jax.nn.silu(gate_pre) * up_pre).astype(jnp.bfloat16)
        result = contract_cols(hidden, down_mat).astype(jnp.bfloat16)
        returned = from_experts(result)
        gate_rows = jnp.where(picks, gate_prob[:, None, :], 0.0).reshape(E * CAP, local_tokens)
        gate_high, gate_low = halves(gate_rows)
        saved.append(
            (
                stream,
                scale_first,
                normed_block,
                queries,
                keys_all,
                attended,
                log_total,
                middle,
                scale_second,
                normed_ffn,
                gate_prob,
                gate_rows,
                returned,
                arrived,
                gate_pre,
                up_pre,
                hidden,
                (attn_mat, router, gain_first, gain_second, out_mat, gate_mat, up_mat, down_mat),
            )
        )
        stream = middle + contract_rows(gate_high, returned) + contract_rows(gate_low, returned)
    grad_stream = cotangent.astype(jnp.float32)
    layer_grads = [None] * LAYERS
    mats_grads = [None] * LAYERS
    out_grads = [None] * LAYERS
    earlier_sums = ()
    for layer_index in range(LAYERS - 1, -1, -1):
        (
            stream_in,
            scale_first,
            normed_block,
            queries,
            keys_all,
            attended,
            log_total,
            middle,
            scale_second,
            normed_ffn,
            gate_prob,
            gate_rows,
            returned,
            arrived,
            gate_pre,
            up_pre,
            hidden,
            (attn_mat, router, gain_first, gain_second, out_mat, gate_mat, up_mat, down_mat),
        ) = saved[layer_index]
        grad_high, grad_low = halves(grad_stream)
        spread = dot(picks_mat, grad_high) + dot(picks_mat, grad_low)
        row_gate = jnp.sum(gate_rows, axis=1, keepdims=True)
        grad_result = to_experts((spread * row_gate).astype(jnp.bfloat16))
        if earlier_sums:
            grad_result, out_grads[layer_index + 1] = lax.optimization_barrier(
                (grad_result, earlier_sums[1])
            )
        row_choice = contract_cols(returned, grad_high) + contract_cols(returned, grad_low)
        grad_choice = jnp.sum(
            jnp.where(picks, row_choice.reshape(E, CAP, local_tokens), 0.0), axis=1
        )
        grad_hidden = dot(grad_result, down_mat)
        gate_sig = jax.nn.sigmoid(gate_pre)
        grad_gate_pre = (
            grad_hidden * up_pre * gate_sig * (1.0 + gate_pre * (1.0 - gate_sig))
        ).astype(jnp.bfloat16)
        grad_up_pre = (grad_hidden * gate_pre * gate_sig).astype(jnp.bfloat16)
        grad_arrived = (
            contract_cols(grad_gate_pre, gate_mat) + contract_cols(grad_up_pre, up_mat)
        ).astype(jnp.bfloat16)
        grad_rows = from_experts(grad_arrived)
        if earlier_sums:
            grad_rows, mats_grads[layer_index + 1] = lax.optimization_barrier(
                (grad_rows, earlier_sums[0])
            )
        down_grads = exchange_grads([contract_rows(grad_result, hidden)])
        gate_up_grads = exchange_grads(
            [contract_rows(arrived, grad_gate_pre), contract_rows(arrived, grad_up_pre)]
        )
        grad_normed = contract_rows(picks_mat, grad_rows)
        grad_logits = gate_prob * (
            grad_choice - jnp.sum(gate_prob * grad_choice, axis=0, keepdims=True)
        )
        grad_normed = grad_normed + lax.dot_general(
            grad_logits,
            router.astype(jnp.float32),
            (((0,), (1,)), ((), ())),
            precision=PRECISE,
        )
        grad_router = lax.dot_general(
            normed_ffn.astype(jnp.float32),
            grad_logits,
            (((0,), (1,)), ((), ())),
            precision=PRECISE,
        )
        grad_middle, grad_gain_second = norm_back(middle, scale_second, gain_second, grad_normed)
        grad_stream = grad_stream + grad_middle
        grad_branch = grad_stream.astype(jnp.bfloat16)
        grad_attended = contract_cols(grad_branch, out_mat).astype(jnp.bfloat16)
        grad_attended = lax.all_to_all(
            grad_attended, "head", split_axis=1, concat_axis=0, tiled=True
        )
        branch_block = lax.all_gather(grad_branch, "head", axis=0, tiled=True)
        grad_query, grad_kv, (down_grads, branch_block) = attend_back(
            queries, keys_all, attended, log_total, grad_attended, (down_grads, branch_block)
        )
        grad_out = contract_rows(attended, branch_block)
        grad_side = jnp.concatenate(
            [grad_router, jnp.zeros((D, 1), jnp.float32), grad_gain_second[:, None]], axis=1
        )
        grad_side = jnp.pad(grad_side, ((0, 0), (0, SIDE - grad_side.shape[1])))
        grad_partial, grad_mats = project_back(
            grad_query, grad_kv, normed_block, attn_mat, gain_first, grad_side
        )
        if layer_index > 0:
            grad_normed = lax.psum_scatter(
                grad_partial, "head", scatter_dimension=0, tiled=True
            )
            grad_normed, gate_up_grads = lax.optimization_barrier((grad_normed, gate_up_grads))
            grad_normed = grad_normed.astype(jnp.float32)
        else:
            grad_normed = sum_over_head(grad_partial)
            grad_normed, gate_up_grads = lax.optimization_barrier((grad_normed, gate_up_grads))
        grad_first = norm_back(stream_in, scale_first, gain_first, grad_normed)[0]
        grad_stream = grad_stream + grad_first
        grad_mats = grad_mats.reshape(D, attn_cols)
        grad_mats = lax.psum_scatter(grad_mats, "blk", scatter_dimension=0, tiled=True)
        grad_out = lax.psum_scatter(
            grad_out.astype(jnp.bfloat16), "blk", scatter_dimension=0, tiled=True
        )
        earlier_sums = (grad_mats, grad_out)
        layer_grads[layer_index] = grad_parts(gate_up_grads) + grad_parts(down_grads)
    mats_grads[0], out_grads[0] = earlier_sums
    mats_grads = jnp.stack(
        [sums.reshape(head_count, shard_rows, qkv_cols + SIDE) for sums in mats_grads], axis=1
    )
    mats_grads = lax.all_to_all(
        mats_grads, "head", split_axis=0, concat_axis=0, tiled=True
    ).astype(jnp.float32)

    def joined(start, stop):
        return jnp.transpose(mats_grads[..., start:stop], (1, 2, 0, 3)).reshape(
            LAYERS, shard_rows, -1
        )

    grad_side = jnp.sum(mats_grads[..., qkv_cols:], axis=0)
    gate_grads, up_grads, down_grads = [
        jnp.stack([layer_grads[layer_index][member] for layer_index in range(LAYERS)])
        for member in range(3)
    ]
    return (
        stream,
        grad_stream,
        joined(0, query_cols),
        joined(query_cols, query_cols + key_cols),
        joined(query_cols + key_cols, qkv_cols),
        jnp.stack(out_grads).astype(jnp.float32),
        grad_side[..., :E],
        grad_side[..., E],
        grad_side[..., E + 1],
        gate_grads,
        up_grads,
        down_grads,
    )


def solution(mesh):
    return jax.shard_map(
        per_device,
        mesh=mesh,
        in_specs=(
            P(("blk", "head"), None),
            P(),
            P(("blk", "head"), None),
            P(None, ("head", "blk"), None),
            P(None, ("head", "blk"), None),
            P(None, ("head", "blk"), None),
            P(None, ("head", "blk"), None),
            P(None, ("head", "blk"), None),
            P(None, ("head", "blk")),
            P(None, ("head", "blk")),
            P(None, "head", "blk", None),
            P(None, "head", "blk", None),
            P(None, "head", "blk", None),
            P(("blk", "head"), None),
        ),
        out_specs=(
            P(("blk", "head"), None),
            P(("blk", "head"), None),
            P(None, ("head", "blk"), None),
            P(None, ("head", "blk"), None),
            P(None, ("head", "blk"), None),
            P(None, ("head", "blk"), None),
            P(None, ("head", "blk"), None),
            P(None, ("head", "blk")),
            P(None, ("head", "blk")),
            P(None, "head", "blk", None),
            P(None, "head", "blk", None),
            P(None, "head", "blk", None),
        ),
        check_vma=False,
    )
```
